256 devices in a mesh: space: 128 (over z, y, x), sub: 2 (over core).
Axes of the slice: x: 4, y: 4, z: 8, core: 2. Of those that a mesh axis runs over, the one named last changes fastest.
Arguments:
- fluid_state: float32 [8, 524288], P(None, 'space'), may hold values from 0 to 1
- sphere_state: float32 [7, 4194304], P(None, 'space'), may hold values from 0 to 1
- sphere_offset: float32 [3, 4194304], P(None, 'space'), may hold values from -1 to 1
- tile_list: int32 [32768, 2], P(('space', 'sub')), may hold values from 0 to 255, as said below
- tile_count: int32 [256], P(('space', 'sub')), may hold values from 32 to 128, as said below
- clump_ids: int32 [4194304], P('space'), may hold values from 0 to 1023, as said below
- clump_state: float32 [6, 131072], P(None, 'space'), may hold values from -6 to 6
- clump_inverse: float32 [4, 131072], P(None, 'space'), may hold values from 0.02 to 0.2
Outputs:
- clump_velocity: float32 [6, 131072], P(None, 'space')
- sphere_velocity: float32 [3, 4194304], P(None, 'space')
The draws below stay inside these ranges and needn't reach their ends.
Inputs may be any that keep to these rules, and one draw needn't show every extreme that they name: `tile_list`: within a domain the 256 slots of its two devices name distinct pairs; the first entry is below 256, the second below 32. `tile_count`: some device's list is full in every draw. `clump_ids`: among the spheres sent to one owner from all domains, each clump id names exactly 32 spheres.
All inputs are finite; a program needn't handle non-finite values.
Results may differ from the reference program's by a relative error of at most 0.0003.
Values sent between devices are 32-bit elements; how exact they have to be, the bound alone decides.
A program may use at most 64 MiB of HBM per device.

```python
import math
import jax
import jax.numpy as jnp
from jax import lax

TILE = 128
SPC = 32
SLOT = 256
FLUID_DEV = 4096
TILES = 128
SPH_DEV = 32768
CL_DEV = 1024
SPHERES = 4194304
CLUMPS = 131072
FLUID = 524288
N_SPACE = 128
N_SUB = 2


def draw_tile_list(key, part):
    fluid_tiles = FLUID_DEV // TILE
    pair_count = SPH_DEV // TILE * fluid_tiles

    def one_domain(domain):
        domain_key = jax.random.fold_in(key, domain)
        middle = 1 + jax.random.permutation(jax.random.fold_in(domain_key, 1), pair_count - 2)[:N_SUB * TILES - 2]
        chosen = jnp.concatenate([jnp.array([0, pair_count - 1], jnp.int32), middle.astype(jnp.int32)])
        chosen = chosen[jax.random.permutation(jax.random.fold_in(domain_key, 2), N_SUB * TILES)]
        return jnp.stack([chosen // fluid_tiles, chosen % fluid_tiles], axis=1)
    domain_lists = jax.vmap(one_domain)(jnp.arange(N_SPACE))
    return domain_lists.reshape(N_SPACE * N_SUB * TILES, 2).astype(jnp.int32)


def draw_tile_count(key, part):
    first_draw = jax.random.randint(jax.random.fold_in(key, 1), (N_SPACE * N_SUB,), 0, TILES * 3 // 4)
    second_draw = jax.random.randint(jax.random.fold_in(key, 2), (N_SPACE * N_SUB,), 0, TILES * 3 // 4)
    counts_drawn = TILES // 4 + first_draw * second_draw // TILES
    busiest = jax.random.randint(jax.random.fold_in(key, 3), (), 0, N_SPACE * N_SUB)
    return jnp.where(jnp.arange(N_SPACE * N_SUB) == busiest, TILES, counts_drawn).astype(jnp.int32)


def draw_clump_ids(key, part):

    def one_owner(owner):
        return jax.random.permutation(jax.random.fold_in(key, owner), SPH_DEV) // SPC
    owner_table = jax.vmap(one_owner)(jnp.arange(N_SPACE))
    return owner_table.reshape(N_SPACE, N_SPACE, SLOT).transpose(1, 0, 2).reshape(SPHERES).astype(jnp.int32)


def shard_levels(key, shape, shards, low, largest):
    gain, own = 1.0, jax.random.fold_in(key, 6)
    for position, shards_of in shards:
        draws = jnp.exp(jax.random.uniform(jax.random.fold_in(own, position), (shards_of,), jnp.float32, low / len(shards), largest / len(shards)))
        gain = gain * jnp.repeat(draws, shape[position] // shards_of).reshape([-1 if axis == position else 1 for axis in range(len(shape))])
    return gain


def noise(key, dims, width, limit, split=(), kind=jnp.bfloat16):
    values = width * jax.random.normal(key, dims, jnp.float32)
    if split:
        values = values * shard_levels(key, dims, split, -0.22, 0.18)
    return jnp.clip(values, -limit, limit).astype(kind)


def setup_inputs(seed: int = 0) -> dict:
    keys = jax.random.split(jax.random.key(seed), 9)
    fluid_state = jnp.clip(1.0 * jax.random.uniform(keys[0], (8, FLUID), jnp.float32) ** shard_levels(keys[0], (8, FLUID), ((1, 128),), -0.2, 0.2), 0.0, 1.0)
    sphere_state = jnp.clip(1.0 * jax.random.uniform(keys[1], (7, SPHERES), jnp.float32) ** shard_levels(keys[1], (7, SPHERES), ((1, 128),), -0.2, 0.2), 0.0, 1.0)
    sphere_offset = jnp.clip(jax.random.uniform(keys[2], (3, SPHERES), jnp.float32, -1.0, 1.0) * shard_levels(keys[2], (3, SPHERES), ((1, 128),), -0.4, 0.0), -1.0, 1.0)
    tile_list = draw_tile_list(jax.random.fold_in(keys[8], 71), 0)
    tile_count = draw_tile_count(jax.random.fold_in(keys[8], 71), 0)
    clump_ids = draw_clump_ids(jax.random.fold_in(keys[8], 71), 0)
    clump_state = noise(keys[6], (6, CLUMPS), 1.0, 6.0, ((1, 128),), jnp.float32)
    clump_inverse = jnp.clip(jnp.exp(math.log(0.2) - 2.3025851 * jax.random.uniform(keys[7], (4, CLUMPS), jnp.float32) ** shard_levels(keys[7], (4, CLUMPS), ((1, 128),), -0.2, 0.2)), 0.02, 0.2)
    return {"fluid_state": fluid_state, "sphere_state": sphere_state, "sphere_offset": sphere_offset, "tile_list": tile_list, "tile_count": tile_count, "clump_ids": clump_ids, "clump_state": clump_state, "clump_inverse": clump_inverse}


support_radius = 0.5
press_coef = 4.0
visc_coef = 1.0
gravity_step = 0.1

def cross_rows(left, right):
    return jnp.stack([left[1] * right[2] - left[2] * right[1], left[2] * right[0] - left[0] * right[2], left[0] * right[1] - left[1] * right[0]], axis=0)

def tile_force(fluid_state, sphere_state, sphere_tile, fluid_tile, tile_width):
    spheres = lax.dynamic_slice_in_dim(sphere_state, (sphere_tile * tile_width).astype(jnp.int32), tile_width, 1)
    fluid = lax.dynamic_slice_in_dim(fluid_state, (fluid_tile * tile_width).astype(jnp.int32), tile_width, 1)
    separation = spheres[0:3, :, None] - fluid[0:3, None, :]
    distance = jnp.sqrt(lax.optimization_barrier(jnp.sum(separation * separation, axis=0)))
    falloff = jnp.maximum(1.0 - distance / support_radius, 0.0)
    weight = falloff * falloff * falloff * fluid[7][None, :]
    pressure = press_coef * (spheres[6][:, None] + fluid[6][None, :]) * weight
    repulsion = lax.optimization_barrier(jnp.sum(pressure[None, :, :] * separation, axis=2))
    drag = lax.optimization_barrier(jnp.sum(weight[None, :, :] * (fluid[3:6, None, :] - spheres[3:6, :, None]), axis=2))
    return repulsion + visc_coef * drag

def add_tile(forces, fluid_state, sphere_state, pair, tile_width):
    term = tile_force(fluid_state, sphere_state, pair[0], pair[1], tile_width)
    first_col = (pair[0] * tile_width).astype(jnp.int32)
    current = lax.dynamic_slice_in_dim(forces, first_col, tile_width, 1)
    return lax.dynamic_update_slice_in_dim(forces, current + term, first_col, 1)

def domain_forces(fluid_state, sphere_state, tile_list, tile_count):
    forces = jnp.zeros((3, SPH_DEV), jnp.float32)
    for sub_core in range(N_SUB):

        def accumulate(entry_number, forces, sub_core=sub_core):
            return add_tile(forces, fluid_state, sphere_state, tile_list[sub_core * TILES + entry_number], TILE)
        forces = lax.fori_loop(0, tile_count[sub_core], accumulate, forces)
    return forces

def reference(fluid_state, sphere_state, sphere_offset, tile_list, tile_count, clump_ids, clump_state, clump_inverse):
    fluid_blocks = fluid_state.reshape(8, N_SPACE, FLUID_DEV).transpose(1, 0, 2)
    sphere_blocks = sphere_state.reshape(7, N_SPACE, SPH_DEV).transpose(1, 0, 2)
    list_blocks = tile_list.reshape(N_SPACE, N_SUB * TILES, 2)
    count_blocks = tile_count.reshape(N_SPACE, N_SUB)
    forces = lax.map(lambda group: domain_forces(group[0], group[1], group[2], group[3]), (fluid_blocks, sphere_blocks, list_blocks, count_blocks))
    forces = forces.transpose(1, 0, 2).reshape(3, SPHERES)
    sphere_loads = jnp.concatenate([forces, cross_rows(sphere_offset, forces)], axis=0)
    owner = jnp.arange(SPHERES, dtype=jnp.int32) // SLOT % N_SPACE
    global_ids = (owner * CL_DEV + clump_ids).astype(jnp.int32)
    totals = jax.ops.segment_sum(sphere_loads.T, global_ids, num_segments=CLUMPS).T
    gravity_pull = jnp.array([0.0, 0.0, -gravity_step], jnp.float32)[:, None]
    linear = clump_state[0:3] + clump_inverse[0:1] * totals[0:3] + gravity_pull
    angular = clump_state[3:6] + clump_inverse[1:4] * totals[3:6]
    clump_velocity = jnp.concatenate([linear, angular], axis=0)
    picked = jnp.take(clump_velocity, global_ids, axis=1)
    sphere_velocity = picked[0:3] + cross_rows(picked[3:6], sphere_offset)
    return (clump_velocity, sphere_velocity)
```

```python
import functools

import jax
import jax.numpy as jnp
from jax import lax
from jax.experimental import pallas as pl
from jax.experimental.pallas import tpu as pltpu
from jax.sharding import PartitionSpec as P

TILE = 128
HI = 8

MESH = pl.DeviceIdType.MESH
f32 = jnp.float32
bf16 = jnp.bfloat16

press_coef = 4.0
gravity_step = 0.1


def split2(x):
    hi = x.astype(bf16).astype(f32)
    return hi, x - hi


def row8(row):
    return jnp.broadcast_to(row, (8, TILE))


def kernel(
    n,
    slots,
    fluid_tiles,
    group,
    tl_s,
    tl_v,
    cnt_s,
    fluid,
    sphere,
    offset,
    ids,
    cstate,
    cinv,
    vel_out,
    sv_out,
    fb,
    fcol,
    terms,
    f_own,
    f_oth,
    f_in,
    send_o,
    recv_o,
    send_f,
    recv_f,
    send_v,
    recv_v,
    part_v,
    hot,
    acc,
    tot_send,
    tot_in,
    cs8,
    vel8,
    by_tile,
    sem_so,
    sem_ro,
    sem_sf,
    sem_rf,
    sem_sv,
    sem_rv,
    sem_ps,
    sem_pr,
    sem_vs,
    sem_vr,
):
    d = lax.axis_index("space")
    s = lax.axis_index("sub")
    other = 1 - s
    groups = n // group

    bar = pltpu.get_barrier_semaphore()

    def greet(k, c):
        pl.semaphore_signal(bar, inc=1, device_id=(lax.rem(d + k, n), s), device_id_type=MESH)
        return c

    lax.fori_loop(1, n, greet, 0)
    pl.semaphore_signal(bar, inc=1, device_id=(d, other), device_id_type=MESH)

    def prep(b, c):
        tile = fluid[:, pl.ds(pl.multiple_of(b * TILE, TILE), TILE)]
        turned = jnp.transpose(tile * 2.0)
        for axis in range(3):
            fb[b, axis] = jnp.broadcast_to(turned[:, axis : axis + 1], (TILE, TILE))
        mass = tile[7:8]
        pm = tile[6:7] * mass
        centred = tile[0:3] - 0.5
        mx = mass * centred
        mv = mass * tile[3:6] - press_coef * (pm * centred)
        zero = jnp.zeros((5, TILE), f32)
        rows = jnp.concatenate(
            [
                jnp.broadcast_to(mass, (3, TILE)), zero,
                jnp.broadcast_to(pm, (3, TILE)), zero,
                mx, zero,
                mv, zero,
            ],
            axis=0,
        )
        hi, lo = split2(rows)
        fcol[b] = jnp.concatenate([hi, lo], axis=0).astype(bf16)
        return c

    lax.fori_loop(0, fluid_tiles, prep, 0)

    def stage_o(o, c):
        tile = 2 * o + s
        send_o[o, 0:3, :] = offset[:, pl.ds(pl.multiple_of(tile * TILE, TILE), TILE)]
        send_o[o, 3:4, :] = ids[pl.ds(tile, 1), :].astype(f32)
        return c

    lax.fori_loop(0, n, stage_o, 0)

    def stage_s(a, c):
        by_tile[a] = sphere[:, pl.ds(pl.multiple_of(a * TILE, TILE), TILE)]
        return c

    lax.fori_loop(0, 2 * n, stage_s, 0)

    for r in range(6):
        for h in range(HI):
            cs8[r, h : h + 1, :] = cstate[r : r + 1, h * TILE : (h + 1) * TILE]
    for r in range(4):
        for h in range(HI):
            cs8[6 + r, h : h + 1, :] = cinv[r : r + 1, h * TILE : (h + 1) * TILE]

    pl.semaphore_wait(bar, n)

    def push_o(k):
        o = lax.rem(d + k, n)
        pltpu.make_async_remote_copy(
            src_ref=send_o.at[o],
            dst_ref=recv_o.at[d],
            send_sem=sem_so,
            recv_sem=sem_ro,
            device_id=(o, s),
            device_id_type=MESH,
        ).start()

    def slot(t):
        a = tl_s[0, t]
        b = tl_s[1, t]
        spheres = by_tile[a]
        twice = spheres[0:3] * 2.0
        sep = twice[0:1] - fb[b, 0]
        d2 = sep * sep
        sep = twice[1:2] - fb[b, 1]
        d2 = d2 + sep * sep
        sep = twice[2:3] - fb[b, 2]
        d2 = d2 + sep * sep
        d2 = jnp.maximum(d2, 1e-30)
        fall = jnp.maximum(1.0 - d2 * lax.rsqrt(d2), 0.0)
        cube = fall * fall * fall
        hi = cube.astype(bf16)
        lo = (cube - hi.astype(f32)).astype(bf16)
        col = fcol[b]
        sums = jnp.dot(
            jnp.concatenate([col, col], axis=1),
            jnp.concatenate([hi, lo], axis=0),
            preferred_element_type=f32,
        )
        sums = sums[0:32] + sums[32:64]
        x3 = spheres[0:3] - 0.5
        p4 = press_coef * spheres[6:7]
        force = (
            sums[0:3] * (p4 * x3 - spheres[3:6])
            + (press_coef * x3) * sums[8:11]
            - p4 * sums[16:19]
            + sums[24:27]
        )
        terms[pl.ds(pl.multiple_of(t * 8, 8), 3), :] = force

    pltpu.make_async_copy(send_o.at[d], recv_o.at[d], sem_ro).start()

    def both(t, c):
        push_o(t)
        slot(t)
        return c

    def only(t, c):
        slot(t)
        return c

    slot(0)
    lax.fori_loop(1, n, both, 0)
    if slots > n:
        lax.fori_loop(n, slots, only, 0)

    lists = tl_v[0:1, :]
    live = lax.broadcasted_iota(jnp.int32, (n, slots), 1) < cnt_s[0]
    tile_row = 2 * lax.broadcasted_iota(jnp.int32, (n, slots), 0)

    def place(parity, out):
        match = jnp.where(
            live & (jnp.broadcast_to(lists, (n, slots)) == tile_row + parity), 1.0, 0.0
        ).astype(bf16)
        for axis in range(3):
            rows = terms[pl.ds(axis, slots, stride=8), :]
            hi, lo = split2(rows)
            out[axis] = jnp.dot(match, hi.astype(bf16), preferred_element_type=f32) + jnp.dot(
                match, lo.astype(bf16), preferred_element_type=f32
            )

    place(other, f_oth)
    swap_f = pltpu.make_async_remote_copy(
        src_ref=f_oth, dst_ref=f_in, send_sem=sem_ps.at[0], recv_sem=sem_pr.at[0],
        device_id=(d, other), device_id_type=MESH,
    )
    swap_f.start()
    place(s, f_own)
    swap_f.wait()

    def stage_f(o):
        for axis in range(3):
            send_f[o, axis : axis + 1, :] = (
                f_own[axis, pl.ds(o, 1), :] + f_in[axis, pl.ds(o, 1), :]
            )

    my_group = d // group

    stage_f(d)
    pltpu.make_async_copy(send_f.at[d], recv_f.at[d], sem_rf.at[my_group]).start()

    def push_f(k, c):
        o = lax.rem(d + k, n)
        stage_f(o)
        pltpu.make_async_remote_copy(
            src_ref=send_f.at[o],
            dst_ref=recv_f.at[d],
            send_sem=sem_sf,
            recv_sem=sem_rf.at[my_group],
            device_id=(o, s),
            device_id_type=MESH,
        ).start()
        return c

    lax.fori_loop(1, n, push_f, 0)

    pltpu.make_async_copy(recv_o, recv_o, sem_ro).wait()
    low_rows = lax.broadcasted_iota(jnp.int32, (TILE, TILE), 0).astype(f32)
    high_rows = lax.broadcasted_iota(jnp.int32, (HI, TILE), 0).astype(f32)

    def high_low(e):
        label = recv_o[e, 3:4, :]
        high = jnp.floor(label * (1.0 / TILE))
        return high, label - high * TILE

    def build(p, c):
        pieces = []
        for e in range(2):
            _, low = high_low(2 * p + e)
            pieces.append(
                jnp.where(jnp.broadcast_to(low, (TILE, TILE)) == low_rows, 1.0, 0.0).astype(bf16)
            )
        hot[p] = jnp.concatenate(pieces, axis=1)
        return c

    lax.fori_loop(0, n // 2, build, 0)

    acc[...] = jnp.zeros_like(acc)

    def spread(e):
        high, _ = high_low(e)
        mask = row8(high) == high_rows
        force = [row8(recv_f[e, r : r + 1, :]) for r in range(3)]
        off = [row8(recv_o[e, r : r + 1, :]) for r in range(3)]
        load = force + [
            off[1] * force[2] - off[2] * force[1],
            off[2] * force[0] - off[0] * force[2],
            off[0] * force[1] - off[1] * force[0],
        ]
        load = [jnp.where(mask, x, 0.0) for x in load]
        parts = [split2(x) for x in load]
        return jnp.concatenate([p[0] for p in parts] + [p[1] for p in parts], axis=0).astype(bf16)

    def gather_in(p, c):
        left = jnp.concatenate([spread(2 * p), spread(2 * p + 1)], axis=1)
        acc[...] += lax.dot_general(
            left, hot[p], (((1,), (1,)), ((), ())), preferred_element_type=f32
        )
        return c

    def group_in(g, c):
        block = recv_f.at[pl.ds(g * group, group)]
        pltpu.make_async_copy(block, block, sem_rf.at[g]).wait()
        lax.fori_loop(g * (group // 2), (g + 1) * (group // 2), gather_in, 0)
        return c

    lax.fori_loop(0, groups, group_in, 0)

    tot_send[...] = acc[0 : 6 * HI, :] + acc[6 * HI : 12 * HI, :]
    swap_t = pltpu.make_async_remote_copy(
        src_ref=tot_send, dst_ref=tot_in, send_sem=sem_ps.at[1], recv_sem=sem_pr.at[1],
        device_id=(d, other), device_id_type=MESH,
    )
    swap_t.start()
    swap_t.wait()

    velocity = []
    for r in range(6):
        total = tot_send[r * HI : (r + 1) * HI, :] + tot_in[r * HI : (r + 1) * HI, :]
        value = cs8[r] + cs8[6 if r < 3 else 4 + r] * total
        if r == 2:
            value = value - gravity_step
        velocity.append(value)
        for h in range(HI):
            vel_out[r : r + 1, h * TILE : (h + 1) * TILE] = value[h : h + 1, :]
    parts = [split2(x) for x in velocity]
    vel8[...] = jnp.concatenate([p[0] for p in parts] + [p[1] for p in parts], axis=0).astype(bf16)

    def stage_v(p):
        got = jnp.dot(vel8[...], hot[p], preferred_element_type=f32)
        got = got[0 : 6 * HI] + got[6 * HI : 12 * HI]
        for half in range(2):
            e = 2 * p + half
            cols = slice(half * TILE, (half + 1) * TILE)
            high, _ = high_low(e)
            mask = row8(high) == high_rows
            mine = [got[r * HI : (r + 1) * HI, cols] for r in range(6)]
            off = [row8(recv_o[e, r : r + 1, :]) for r in range(3)]
            for r in range(3):
                r1, r2 = (r + 1) % 3, (r + 2) % 3
                value = mine[r] + mine[3 + r1] * off[r2] - mine[3 + r2] * off[r1]
                send_v[e, r : r + 1, :] = jnp.sum(
                    jnp.where(mask, value, 0.0), axis=0, keepdims=True
                )

    def send_back(e):
        pltpu.make_async_remote_copy(
            src_ref=send_v.at[e],
            dst_ref=recv_v.at[d],
            send_sem=sem_sv,
            recv_sem=sem_rv.at[my_group],
            device_id=(e, s),
            device_id_type=MESH,
        ).start()

    my_pair = d // 2

    def push_v(k, c):
        p = lax.rem(my_pair + k, n // 2)
        stage_v(p)
        send_back(2 * p)
        send_back(2 * p + 1)
        return c

    lax.fori_loop(1, n // 2, push_v, 0)
    stage_v(my_pair)
    send_back(d + 1 - 2 * lax.rem(d, 2))
    pltpu.make_async_copy(send_v.at[d], recv_v.at[d], sem_rv.at[my_group]).start()

    def swap_v(g):
        block = pl.ds(g * group, group)
        return pltpu.make_async_remote_copy(
            src_ref=recv_v.at[block], dst_ref=part_v.at[block],
            send_sem=sem_vs, recv_sem=sem_vr.at[g],
            device_id=(d, other), device_id_type=MESH,
        )

    def write(parity, ref, o, c):
        first = pl.multiple_of((2 * o + parity) * TILE, TILE)
        sv_out[:, pl.ds(first, TILE)] = ref[o]
        return c

    def group_v(g, c):
        block = recv_v.at[pl.ds(g * group, group)]
        pltpu.make_async_copy(block, block, sem_rv.at[g]).wait()
        swap_v(g).start()
        lax.fori_loop(g * group, (g + 1) * group, functools.partial(write, s, recv_v), 0)
        return c

    lax.fori_loop(0, groups, group_v, 0)

    def group_p(g, c):
        block = part_v.at[pl.ds(g * group, group)]
        pltpu.make_async_copy(block, block, sem_vr.at[g]).wait()
        lax.fori_loop(g * group, (g + 1) * group, functools.partial(write, other, part_v), 0)
        return c

    lax.fori_loop(0, groups, group_p, 0)

    for ref, sem in ((send_o, sem_so), (send_f, sem_sf), (send_v, sem_sv)):
        block = ref.at[pl.ds(0, n - 1)]
        pltpu.make_async_copy(block, block, sem).wait()
    pltpu.make_async_copy(recv_v, recv_v, sem_vs).wait()


def per_device(
    fluid_state,
    sphere_state,
    sphere_offset,
    tile_list,
    tile_count,
    clump_ids,
    clump_state,
    clump_inverse,
):
    n = lax.axis_size("space")
    slots = tile_list.shape[0]
    fluid_tiles = fluid_state.shape[1] // TILE
    spheres = sphere_state.shape[1]
    clumps = clump_state.shape[1]
    group = 16 if n >= 32 else 2
    groups = n // group
    lists = tile_list.T
    vmem = pl.BlockSpec(memory_space=pltpu.VMEM)
    smem = pl.BlockSpec(memory_space=pltpu.SMEM)
    dma = pltpu.SemaphoreType.DMA
    return pl.pallas_call(
        functools.partial(kernel, n, slots, fluid_tiles, group),
        out_shape=(
            jax.ShapeDtypeStruct((6, clumps), f32),
            jax.ShapeDtypeStruct((3, spheres), f32),
        ),
        in_specs=[smem, vmem, smem] + [vmem] * 6,
        out_specs=(vmem, vmem),
        scratch_shapes=[
            pltpu.VMEM((fluid_tiles, 3, TILE, TILE), f32),
            pltpu.VMEM((fluid_tiles, 64, TILE), bf16),
            pltpu.VMEM((slots * 8, TILE), f32),
            pltpu.VMEM((3, n, TILE), f32),
            pltpu.VMEM((3, n, TILE), f32),
            pltpu.VMEM((3, n, TILE), f32),
            pltpu.VMEM((n, 4, TILE), f32),
            pltpu.VMEM((n, 4, TILE), f32),
            pltpu.VMEM((n, 3, TILE), f32),
            pltpu.VMEM((n, 3, TILE), f32),
            pltpu.VMEM((n, 3, TILE), f32),
            pltpu.VMEM((n, 3, TILE), f32),
            pltpu.VMEM((n, 3, TILE), f32),
            pltpu.VMEM((n // 2, TILE, 2 * TILE), bf16),
            pltpu.VMEM((12 * HI, TILE), f32),
            pltpu.VMEM((6 * HI, TILE), f32),
            pltpu.VMEM((6 * HI, TILE), f32),
            pltpu.VMEM((10, HI, TILE), f32),
            pltpu.VMEM((12 * HI, TILE), bf16),
            pltpu.VMEM((2 * n, 7, TILE), f32),
            dma(()),
            dma(()),
            dma(()),
            dma((groups,)),
            dma(()),
            dma((groups,)),
            dma((2,)),
            dma((2,)),
            dma(()),
            dma((groups,)),
        ],
        compiler_params=pltpu.CompilerParams(
            collective_id=0, has_side_effects=True, vmem_limit_bytes=40 << 20
        ),
        name="step",
    )(
        lists,
        lists,
        tile_count,
        fluid_state,
        sphere_state,
        sphere_offset,
        clump_ids.reshape(spheres // TILE, TILE),
        clump_state,
        clump_inverse,
    )


def solution(mesh):
    in_specs = (
        P(None, "space"),
        P(None, "space"),
        P(None, "space"),
        P(("space", "sub"), None),
        P(("space", "sub")),
        P("space"),
        P(None, "space"),
        P(None, "space"),
    )
    out_specs = (P(None, "space"), P(None, "space"))
    return jax.shard_map(
        per_device, mesh=mesh, in_specs=in_specs, out_specs=out_specs, check_vma=False
    )
```

```python
import functools

import jax
import jax.numpy as jnp
from jax import lax
from jax.experimental import pallas as pl
from jax.experimental.pallas import tpu as pltpu
from jax.sharding import PartitionSpec as P

TILE = 128
SLOT_UNROLL = 16
PREP_UNROLL = 4
HI = 8

MESH = pl.DeviceIdType.MESH
f32 = jnp.float32
bf16 = jnp.bfloat16

press_coef = 4.0
gravity_step = 0.1


def split2(x):
    hi = x.astype(bf16).astype(f32)
    return hi, x - hi


def row8(row):
    return jnp.broadcast_to(row, (8, TILE))


def kernel(
    n,
    slots,
    fluid_tiles,
    group,
    tl_h,
    cnt_s,
    fluid_h,
    sphere_h,
    offset_h,
    ids_h,
    cstate_h,
    cinv_h,
    vel_out,
    sv_out,
    tl_s,
    tl_v,
    fluid,
    sphere,
    offset,
    ids,
    cstate,
    cinv,
    fb,
    fcol,
    by_tile,
    terms,
    f_own,
    f_oth,
    f_in,
    send_o,
    recv_o,
    send_f,
    recv_f,
    send_v,
    recv_v,
    part_v,
    hot,
    tot_send,
    tot_in,
    cs8,
    vel8,
    sem_in,
    sem_so,
    sem_ro,
    sem_sf,
    sem_rf,
    sem_sv,
    sem_rv,
    sem_ps,
    sem_pr,
    sem_vs,
    sem_vr,
):
    d = lax.axis_index("space")
    s = lax.axis_index("sub")
    other = 1 - s
    groups = n // group
    my_group = d // group
    place_in_group = lax.rem(d, group)

    loads = [
        pltpu.make_async_copy(src, dst, sem_in.at[i])
        for i, (src, dst) in enumerate(
            [
                (fluid_h, fluid),
                (sphere_h, sphere),
                (tl_h, tl_s),
                (offset_h, offset),
                (ids_h, ids),
                (tl_h, tl_v),
                (cstate_h, cstate),
                (cinv_h, cinv),
            ]
        )
    ]
    for copy in loads:
        copy.start()

    bar = pltpu.get_barrier_semaphore()

    def greet(k, c):
        pl.semaphore_signal(bar, inc=1, device_id=(lax.rem(d + k, n), s), device_id_type=MESH)
        return c

    pl.semaphore_signal(bar, inc=1, device_id=(d, other), device_id_type=MESH)
    lax.fori_loop(1, n, greet, 0)

    loads[0].wait()

    def prep(b, c):
        tile = fluid[:, pl.ds(pl.multiple_of(b * TILE, TILE), TILE)]
        turned = jnp.transpose(tile * 2.0)
        for axis in range(3):
            fb[b, axis] = jnp.broadcast_to(turned[:, axis : axis + 1], (TILE, TILE))
        mass = tile[7:8]
        pm = tile[6:7] * mass
        centred = tile[0:3] - 0.5
        mx = mass * centred
        mv = mass * tile[3:6] - press_coef * (pm * centred)
        zero = jnp.zeros((5, TILE), f32)
        rows = jnp.concatenate(
            [
                jnp.broadcast_to(mass, (3, TILE)), zero,
                jnp.broadcast_to(pm, (3, TILE)), zero,
                mx, zero,
                mv, zero,
            ],
            axis=0,
        )
        hi, lo = split2(rows)
        fcol[b] = jnp.concatenate([hi, lo], axis=0).astype(bf16)
        return c

    lax.fori_loop(0, fluid_tiles, prep, 0, unroll=PREP_UNROLL)

    loads[1].wait()

    def stage_s(a, c):
        by_tile[a] = sphere[:, pl.ds(pl.multiple_of(a * TILE, TILE), TILE)]
        return c

    lax.fori_loop(0, 2 * n, stage_s, 0, unroll=8)

    loads[3].wait()
    loads[4].wait()

    def stage_o(o, c):
        tile = 2 * o + s
        send_o[o, 0:3, :] = offset[:, pl.ds(pl.multiple_of(tile * TILE, TILE), TILE)]
        send_o[o, 3:4, :] = ids[pl.ds(tile, 1), :].astype(f32)
        return c

    lax.fori_loop(0, n, stage_o, 0, unroll=min(n, 8))

    for i in (2, 5, 6, 7):
        loads[i].wait()

    pl.semaphore_wait(bar, n)

    pltpu.make_async_copy(send_o.at[d], recv_o.at[d], sem_ro).start()

    def push_o(k, c):
        o = lax.rem(d + k, n)
        pltpu.make_async_remote_copy(
            src_ref=send_o.at[o],
            dst_ref=recv_o.at[d],
            send_sem=sem_so,
            recv_sem=sem_ro,
            device_id=(o, s),
            device_id_type=MESH,
        ).start()
        return c

    lax.fori_loop(1, n, push_o, 0)

    def slot(t, c):
        a = tl_s[0, t]
        b = tl_s[1, t]
        spheres = by_tile[a]
        twice = spheres[0:3] * 2.0
        sep = twice[0:1] - fb[b, 0]
        d2 = sep * sep
        sep = twice[1:2] - fb[b, 1]
        d2 = d2 + sep * sep
        sep = twice[2:3] - fb[b, 2]
        d2 = d2 + sep * sep
        d2 = jnp.maximum(d2, 1e-30)
        fall = jnp.maximum(1.0 - d2 * lax.rsqrt(d2), 0.0)
        cube = fall * fall * fall
        hi = cube.astype(bf16)
        lo = (cube - hi.astype(f32)).astype(bf16)
        col = fcol[b]
        sums = jnp.dot(
            jnp.concatenate([col, col], axis=1),
            jnp.concatenate([hi, lo], axis=0),
            preferred_element_type=f32,
        )
        sums = sums[0:32] + sums[32:64]
        x3 = spheres[0:3] - 0.5
        p4 = press_coef * spheres[6:7]
        force = (
            sums[0:3] * (p4 * x3 - spheres[3:6])
            + (press_coef * x3) * sums[8:11]
            - p4 * sums[16:19]
            + sums[24:27]
        )
        terms[pl.ds(pl.multiple_of(t * 8, 8), 3), :] = force
        return c

    lax.fori_loop(0, slots, slot, 0, unroll=min(slots, SLOT_UNROLL))

    lists = tl_v[0:1, :]
    live = lax.broadcasted_iota(jnp.int32, (n, slots), 1) < cnt_s[0]
    tile_row = 2 * lax.broadcasted_iota(jnp.int32, (n, slots), 0)

    def place(parity, out):
        match = jnp.where(
            live & (jnp.broadcast_to(lists, (n, slots)) == tile_row + parity), 1.0, 0.0
        ).astype(bf16)
        for axis in range(3):
            rows = terms[pl.ds(axis, slots, stride=8), :]
            hi, lo = split2(rows)
            out[axis] = jnp.dot(match, hi.astype(bf16), preferred_element_type=f32) + jnp.dot(
                match, lo.astype(bf16), preferred_element_type=f32
            )

    place(other, f_oth)
    swap_f = pltpu.make_async_remote_copy(
        src_ref=f_oth, dst_ref=f_in, send_sem=sem_ps.at[0], recv_sem=sem_pr.at[0],
        device_id=(d, other), device_id_type=MESH,
    )
    swap_f.start()
    place(s, f_own)
    swap_f.wait()

    def stage_f(o, c):
        for axis in range(3):
            send_f[o, axis : axis + 1, :] = (
                f_own[axis, pl.ds(o, 1), :] + f_in[axis, pl.ds(o, 1), :]
            )
        return c

    lax.fori_loop(0, n, stage_f, 0, unroll=min(n, 8))

    def push_f(k, c):
        o = lax.rem(d + k, n)
        pltpu.make_async_remote_copy(
            src_ref=send_f.at[o],
            dst_ref=recv_f.at[d],
            send_sem=sem_sf,
            recv_sem=sem_rf.at[my_group],
            device_id=(o, s),
            device_id_type=MESH,
        ).start()
        return c

    lax.fori_loop(1, n, push_f, 0)
    pltpu.make_async_copy(send_f.at[d], recv_f.at[d], sem_rf.at[my_group]).start()

    for r in range(6):
        for h in range(HI):
            cs8[r, h : h + 1, :] = cstate[r : r + 1, h * TILE : (h + 1) * TILE]
    for r in range(4):
        for h in range(HI):
            cs8[6 + r, h : h + 1, :] = cinv[r : r + 1, h * TILE : (h + 1) * TILE]

    pltpu.make_async_copy(recv_o, recv_o, sem_ro).wait()
    low_rows = lax.broadcasted_iota(jnp.int32, (TILE, TILE), 0).astype(f32)
    high_rows = lax.broadcasted_iota(jnp.int32, (HI, TILE), 0).astype(f32)

    def high_low(e):
        label = recv_o[e, 3:4, :]
        high = jnp.floor(label * (1.0 / TILE))
        return high, label - high * TILE

    def build(p, c):
        pieces = []
        for e in range(2):
            _, low = high_low(2 * p + e)
            pieces.append(
                jnp.where(jnp.broadcast_to(low, (TILE, TILE)) == low_rows, 1.0, 0.0).astype(bf16)
            )
        hot[p] = jnp.concatenate(pieces, axis=1)
        return c

    lax.fori_loop(0, n // 2, build, 0, unroll=2)

    def spread(e):
        high, _ = high_low(e)
        mask = row8(high) == high_rows
        force = [row8(recv_f[e, r : r + 1, :]) for r in range(3)]
        off = [row8(recv_o[e, r : r + 1, :]) for r in range(3)]
        load = force + [
            off[1] * force[2] - off[2] * force[1],
            off[2] * force[0] - off[0] * force[2],
            off[0] * force[1] - off[1] * force[0],
        ]
        load = [jnp.where(mask, x, 0.0) for x in load]
        parts = [split2(x) for x in load]
        return jnp.concatenate([p[0] for p in parts] + [p[1] for p in parts], axis=0).astype(bf16)

    def group_in(g, acc):
        block = recv_f.at[pl.ds(g * group, group)]
        pltpu.make_async_copy(block, block, sem_rf.at[g]).wait()
        for i in range(group // 2):
            p = g * (group // 2) + i
            left = jnp.concatenate([spread(2 * p), spread(2 * p + 1)], axis=1)
            acc = acc + lax.dot_general(
                left, hot[p], (((1,), (1,)), ((), ())), preferred_element_type=f32
            )
        return acc

    acc = lax.fori_loop(0, groups, group_in, jnp.zeros((12 * HI, TILE), f32))

    tot_send[...] = acc[0 : 6 * HI, :] + acc[6 * HI : 12 * HI, :]
    swap_t = pltpu.make_async_remote_copy(
        src_ref=tot_send, dst_ref=tot_in, send_sem=sem_ps.at[1], recv_sem=sem_pr.at[1],
        device_id=(d, other), device_id_type=MESH,
    )
    swap_t.start()
    swap_t.wait()

    velocity = []
    for r in range(6):
        total = tot_send[r * HI : (r + 1) * HI, :] + tot_in[r * HI : (r + 1) * HI, :]
        value = cs8[r] + cs8[6 if r < 3 else 4 + r] * total
        if r == 2:
            value = value - gravity_step
        velocity.append(value)
        for h in range(HI):
            vel_out[r : r + 1, h * TILE : (h + 1) * TILE] = value[h : h + 1, :]
    parts = [split2(x) for x in velocity]
    vel8[...] = jnp.concatenate([p[0] for p in parts] + [p[1] for p in parts], axis=0).astype(bf16)

    def stage_v(p):
        got = jnp.dot(vel8[...], hot[p], preferred_element_type=f32)
        got = got[0 : 6 * HI] + got[6 * HI : 12 * HI]
        for half in range(2):
            e = 2 * p + half
            cols = slice(half * TILE, (half + 1) * TILE)
            high, _ = high_low(e)
            mask = row8(high) == high_rows
            mine = [got[r * HI : (r + 1) * HI, cols] for r in range(6)]
            off = [row8(recv_o[e, r : r + 1, :]) for r in range(3)]
            for r in range(3):
                r1, r2 = (r + 1) % 3, (r + 2) % 3
                value = mine[r] + mine[3 + r1] * off[r2] - mine[3 + r2] * off[r1]
                send_v[e, r : r + 1, :] = jnp.sum(
                    jnp.where(mask, value, 0.0), axis=0, keepdims=True
                )

    def stage_group(g):
        for i in range(group // 2):
            stage_v(g * (group // 2) + i)

    def send_back(e):
        pltpu.make_async_remote_copy(
            src_ref=send_v.at[e],
            dst_ref=recv_v.at[d],
            send_sem=sem_sv,
            recv_sem=sem_rv.at[my_group],
            device_id=(e, s),
            device_id_type=MESH,
        ).start()

    def push_v(k, c):
        g = lax.rem(my_group + k, groups)
        stage_group(g)

        def one(i, c):
            send_back(g * group + lax.rem(place_in_group + i, group))
            return c

        return lax.fori_loop(0, group, one, c)

    lax.fori_loop(1, groups, push_v, 0)
    stage_group(my_group)

    def last(i, c):
        send_back(my_group * group + lax.rem(place_in_group + i, group))
        return c

    lax.fori_loop(1, group, last, 0)
    pltpu.make_async_copy(send_v.at[d], recv_v.at[d], sem_rv.at[my_group]).start()

    def swap_v(g):
        block = pl.ds(g * group, group)
        return pltpu.make_async_remote_copy(
            src_ref=recv_v.at[block], dst_ref=part_v.at[block],
            send_sem=sem_vs, recv_sem=sem_vr.at[g],
            device_id=(d, other), device_id_type=MESH,
        )

    def write(parity, ref, g):
        for i in range(group):
            o = g * group + i
            first = pl.multiple_of((2 * o + parity) * TILE, TILE)
            sv_out[:, pl.ds(first, TILE)] = ref[o]

    def group_v(g, c):
        block = recv_v.at[pl.ds(g * group, group)]
        pltpu.make_async_copy(block, block, sem_rv.at[g]).wait()
        swap_v(g).start()
        write(s, recv_v, g)
        return c

    lax.fori_loop(0, groups, group_v, 0)

    def group_p(g, c):
        block = part_v.at[pl.ds(g * group, group)]
        pltpu.make_async_copy(block, block, sem_vr.at[g]).wait()
        write(other, part_v, g)
        return c

    lax.fori_loop(0, groups, group_p, 0)

    for ref, sem in ((send_o, sem_so), (send_f, sem_sf), (send_v, sem_sv)):
        block = ref.at[pl.ds(0, n - 1)]
        pltpu.make_async_copy(block, block, sem).wait()
    pltpu.make_async_copy(recv_v, recv_v, sem_vs).wait()


def per_device(
    fluid_state,
    sphere_state,
    sphere_offset,
    tile_list,
    tile_count,
    clump_ids,
    clump_state,
    clump_inverse,
):
    n = lax.axis_size("space")
    slots = tile_list.shape[0]
    fluid_tiles = fluid_state.shape[1] // TILE
    spheres = sphere_state.shape[1]
    clumps = clump_state.shape[1]
    group = 16 if n >= 32 else 2
    groups = n // group
    lists = tile_list.T
    vmem = pl.BlockSpec(memory_space=pltpu.VMEM)
    hbm = pl.BlockSpec(memory_space=pltpu.HBM)
    dma = pltpu.SemaphoreType.DMA
    block3 = pltpu.VMEM((n, 3, TILE), f32)
    block4 = pltpu.VMEM((n, 4, TILE), f32)
    planes = pltpu.VMEM((3, n, TILE), f32)
    return pl.pallas_call(
        functools.partial(kernel, n, slots, fluid_tiles, group),
        out_shape=(
            jax.ShapeDtypeStruct((6, clumps), f32),
            jax.ShapeDtypeStruct((3, spheres), f32),
        ),
        in_specs=[hbm, pl.BlockSpec(memory_space=pltpu.SMEM)] + [hbm] * 6,
        out_specs=(vmem, vmem),
        scratch_shapes=[
            pltpu.SMEM((2, slots), jnp.int32),
            pltpu.VMEM((2, slots), jnp.int32),
            pltpu.VMEM(fluid_state.shape, f32),
            pltpu.VMEM(sphere_state.shape, f32),
            pltpu.VMEM(sphere_offset.shape, f32),
            pltpu.VMEM((spheres // TILE, TILE), jnp.int32),
            pltpu.VMEM(clump_state.shape, f32),
            pltpu.VMEM(clump_inverse.shape, f32),
            pltpu.VMEM((fluid_tiles, 3, TILE, TILE), f32),
            pltpu.VMEM((fluid_tiles, 64, TILE), bf16),
            pltpu.VMEM((2 * n, 7, TILE), f32),
            pltpu.VMEM((slots * 8, TILE), f32),
            planes,
            planes,
            planes,
            block4,
            block4,
            block3,
            block3,
            block3,
            block3,
            block3,
            pltpu.VMEM((n // 2, TILE, 2 * TILE), bf16),
            pltpu.VMEM((6 * HI, TILE), f32),
            pltpu.VMEM((6 * HI, TILE), f32),
            pltpu.VMEM((10, HI, TILE), f32),
            pltpu.VMEM((12 * HI, TILE), bf16),
            dma((8,)),
            dma(()),
            dma(()),
            dma(()),
            dma((groups,)),
            dma(()),
            dma((groups,)),
            dma((2,)),
            dma((2,)),
            dma(()),
            dma((groups,)),
        ],
        compiler_params=pltpu.CompilerParams(
            collective_id=0, has_side_effects=True, vmem_limit_bytes=56 << 20
        ),
        name="step",
    )(
        lists,
        tile_count,
        fluid_state,
        sphere_state,
        sphere_offset,
        clump_ids.reshape(spheres // TILE, TILE),
        clump_state,
        clump_inverse,
    )


def solution(mesh):
    in_specs = (
        P(None, "space"),
        P(None, "space"),
        P(None, "space"),
        P(("space", "sub"), None),
        P(("space", "sub")),
        P("space"),
        P(None, "space"),
        P(None, "space"),
    )
    out_specs = (P(None, "space"), P(None, "space"))
    return jax.shard_map(
        per_device, mesh=mesh, in_specs=in_specs, out_specs=out_specs, check_vma=False
    )
```

```python
import functools

import jax
import jax.numpy as jnp
from jax import lax
from jax.experimental import pallas as pl
from jax.experimental.pallas import tpu as pltpu
from jax.sharding import PartitionSpec as P

TILE = 128
SLOT_UNROLL = 16
PREP_UNROLL = 4
HI = 8

MESH = pl.DeviceIdType.MESH
f32 = jnp.float32
bf16 = jnp.bfloat16

press_coef = 4.0
gravity_step = 0.1


def split2(x):
    hi = x.astype(bf16).astype(f32)
    return hi, x - hi


def row8(row):
    return jnp.broadcast_to(row, (8, TILE))


def kernel(
    n,
    slots,
    fluid_tiles,
    inner,
    tl_h,
    cnt_s,
    fluid_h,
    sphere_h,
    offset_h,
    ids_h,
    cstate_h,
    cinv_h,
    vel_out,
    sv_out,
    tl_s,
    tl_v,
    fluid,
    sphere,
    offset,
    ids,
    cstate,
    cinv,
    fb,
    fcol,
    by_tile,
    terms,
    f_own,
    f_oth,
    f_in,
    send_o,
    recv_o,
    send_f,
    recv_f,
    send_v,
    recv_v,
    part_v,
    hot,
    tot_send,
    tot_in,
    cs8,
    vel8,
    sem_line,
    sem_in,
    sem_so,
    sem_ro,
    sem_sf,
    sem_rf,
    sem_sv,
    sem_rv,
    sem_ps,
    sem_pr,
    sem_vs,
    sem_vr,
):
    d = lax.axis_index("space")
    s = lax.axis_index("sub")
    other = 1 - s
    planes = n // inner
    pairs = inner // 2
    group = 2 * planes
    my_plane = d // inner
    my_pair = lax.rem(d, inner) // 2
    my_bit = lax.rem(d, 2)
    my_slot = my_pair * group + my_plane * 2 + my_bit

    def peer(k):
        chunk, step = k // group, lax.rem(k, group)
        turn = step // 2
        away = ((turn + 1) // 2) * (1 - 2 * lax.rem(turn + 1, 2))
        return (
            lax.rem(my_plane + away + planes, planes),
            lax.rem(my_pair + chunk, pairs),
            lax.rem(my_bit + lax.rem(step, 2), 2),
        )

    def domain(plane, pair, bit):
        return plane * inner + 2 * pair + bit

    loads = [
        pltpu.make_async_copy(src, dst, sem_in.at[i])
        for i, (src, dst) in enumerate(
            [
                (fluid_h, fluid),
                (sphere_h, sphere),
                (tl_h, tl_s),
                (offset_h, offset),
                (ids_h, ids),
                (tl_h, tl_v),
                (cstate_h, cstate),
                (cinv_h, cinv),
            ]
        )
    ]
    for copy in loads:
        copy.start()

    bar = pltpu.get_barrier_semaphore()

    def greet_plane(k, c):
        mate = my_plane * inner + lax.rem(lax.rem(d, inner) + k, inner)
        pl.semaphore_signal(bar, inc=1, device_id=(mate, s), device_id_type=MESH)
        return c

    def line(k):
        return lax.rem(d + k * inner, n)

    def greet_line(k, c):
        pl.semaphore_signal(bar, inc=1, device_id=(line(k), s), device_id_type=MESH)
        return c

    def vouch(k, c):
        pl.semaphore_signal(sem_line, inc=1, device_id=(line(k), s), device_id_type=MESH)
        return c

    lax.fori_loop(1, planes, greet_line, 0)
    lax.fori_loop(1, inner, greet_plane, 0)
    pl.semaphore_signal(bar, inc=1, device_id=(d, other), device_id_type=MESH)

    loads[0].wait()

    def prep(b, c):
        tile = fluid[:, pl.ds(pl.multiple_of(b * TILE, TILE), TILE)]
        turned = jnp.transpose(tile * 2.0)
        for axis in range(3):
            fb[b, axis] = jnp.broadcast_to(turned[:, axis : axis + 1], (TILE, TILE))
        mass = tile[7:8]
        pm = tile[6:7] * mass
        centred = tile[0:3] - 0.5
        mx = mass * centred
        mv = mass * tile[3:6] - press_coef * (pm * centred)
        zero = jnp.zeros((5, TILE), f32)
        rows = jnp.concatenate(
            [
                jnp.broadcast_to(mass, (3, TILE)), zero,
                jnp.broadcast_to(pm, (3, TILE)), zero,
                mx, zero,
                mv, zero,
            ],
            axis=0,
        )
        hi, lo = split2(rows)
        fcol[b] = jnp.concatenate([hi, lo], axis=0).astype(bf16)
        return c

    lax.fori_loop(0, fluid_tiles, prep, 0, unroll=PREP_UNROLL)

    pl.semaphore_wait(bar, planes + inner - 1)
    lax.fori_loop(1, planes, vouch, 0)

    loads[1].wait()

    def stage_s(a, c):
        by_tile[a] = sphere[:, pl.ds(pl.multiple_of(a * TILE, TILE), TILE)]
        return c

    lax.fori_loop(0, 2 * n, stage_s, 0, unroll=8)

    loads[3].wait()
    loads[4].wait()

    def stage_o(o, c):
        tile = 2 * o + s
        send_o[o, 0:3, :] = offset[:, pl.ds(pl.multiple_of(tile * TILE, TILE), TILE)]
        send_o[o, 3:4, :] = ids[pl.ds(tile, 1), :].astype(f32)
        return c

    lax.fori_loop(0, n, stage_o, 0, unroll=min(n, 8))

    for i in (2, 5, 6, 7):
        loads[i].wait()

    pl.semaphore_wait(sem_line, planes - 1)

    pltpu.make_async_copy(send_o.at[d], recv_o.at[my_slot], sem_ro).start()

    def push_o(k, c):
        o = domain(*peer(k))
        pltpu.make_async_remote_copy(
            src_ref=send_o.at[o],
            dst_ref=recv_o.at[my_slot],
            send_sem=sem_so,
            recv_sem=sem_ro,
            device_id=(o, s),
            device_id_type=MESH,
        ).start()
        return c

    lax.fori_loop(1, n, push_o, 0)

    def slot(t, c):
        a = tl_s[0, t]
        b = tl_s[1, t]
        spheres = by_tile[a]
        twice = spheres[0:3] * 2.0
        sep = twice[0:1] - fb[b, 0]
        d2 = sep * sep
        sep = twice[1:2] - fb[b, 1]
        d2 = d2 + sep * sep
        sep = twice[2:3] - fb[b, 2]
        d2 = d2 + sep * sep
        d2 = jnp.maximum(d2, 1e-30)
        fall = jnp.maximum(1.0 - d2 * lax.rsqrt(d2), 0.0)
        cube = fall * fall * fall
        hi = cube.astype(bf16)
        lo = (cube - hi.astype(f32)).astype(bf16)
        col = fcol[b]
        sums = jnp.dot(
            jnp.concatenate([col, col], axis=1),
            jnp.concatenate([hi, lo], axis=0),
            preferred_element_type=f32,
        )
        sums = sums[0:32] + sums[32:64]
        x3 = spheres[0:3] - 0.5
        p4 = press_coef * spheres[6:7]
        force = (
            sums[0:3] * (p4 * x3 - spheres[3:6])
            + (press_coef * x3) * sums[8:11]
            - p4 * sums[16:19]
            + sums[24:27]
        )
        terms[pl.ds(pl.multiple_of(t * 8, 8), 3), :] = force
        return c

    lax.fori_loop(0, slots, slot, 0, unroll=min(slots, SLOT_UNROLL))

    lists = tl_v[0:1, :]
    live = lax.broadcasted_iota(jnp.int32, (n, slots), 1) < cnt_s[0]
    tile_row = 2 * lax.broadcasted_iota(jnp.int32, (n, slots), 0)

    def place(parity, out):
        match = jnp.where(
            live & (jnp.broadcast_to(lists, (n, slots)) == tile_row + parity), 1.0, 0.0
        ).astype(bf16)
        for axis in range(3):
            rows = terms[pl.ds(axis, slots, stride=8), :]
            hi, lo = split2(rows)
            out[axis] = jnp.dot(match, hi.astype(bf16), preferred_element_type=f32) + jnp.dot(
                match, lo.astype(bf16), preferred_element_type=f32
            )

    place(other, f_oth)
    swap_f = pltpu.make_async_remote_copy(
        src_ref=f_oth, dst_ref=f_in, send_sem=sem_ps.at[0], recv_sem=sem_pr.at[0],
        device_id=(d, other), device_id_type=MESH,
    )
    swap_f.start()
    place(s, f_own)
    swap_f.wait()

    def stage_f(o, c):
        for axis in range(3):
            send_f[o, axis : axis + 1, :] = (
                f_own[axis, pl.ds(o, 1), :] + f_in[axis, pl.ds(o, 1), :]
            )
        return c

    lax.fori_loop(0, n, stage_f, 0, unroll=min(n, 8))

    def push_f(k, c):
        o = domain(*peer(k))
        pltpu.make_async_remote_copy(
            src_ref=send_f.at[o],
            dst_ref=recv_f.at[my_slot],
            send_sem=sem_sf,
            recv_sem=sem_rf.at[my_pair],
            device_id=(o, s),
            device_id_type=MESH,
        ).start()
        return c

    lax.fori_loop(1, n, push_f, 0)
    pltpu.make_async_copy(send_f.at[d], recv_f.at[my_slot], sem_rf.at[my_pair]).start()

    for r in range(6):
        for h in range(HI):
            cs8[r, h : h + 1, :] = cstate[r : r + 1, h * TILE : (h + 1) * TILE]
    for r in range(4):
        for h in range(HI):
            cs8[6 + r, h : h + 1, :] = cinv[r : r + 1, h * TILE : (h + 1) * TILE]

    pltpu.make_async_copy(recv_o, recv_o, sem_ro).wait()
    low_rows = lax.broadcasted_iota(jnp.int32, (TILE, TILE), 0).astype(f32)
    high_rows = lax.broadcasted_iota(jnp.int32, (HI, TILE), 0).astype(f32)

    def high_low(e):
        label = recv_o[e, 3:4, :]
        high = jnp.floor(label * (1.0 / TILE))
        return high, label - high * TILE

    def build(p, c):
        pieces = []
        for e in range(2):
            _, low = high_low(2 * p + e)
            pieces.append(
                jnp.where(jnp.broadcast_to(low, (TILE, TILE)) == low_rows, 1.0, 0.0).astype(bf16)
            )
        hot[p] = jnp.concatenate(pieces, axis=1)
        return c

    lax.fori_loop(0, n // 2, build, 0, unroll=2)

    def spread(e):
        high, _ = high_low(e)
        mask = row8(high) == high_rows
        force = [row8(recv_f[e, r : r + 1, :]) for r in range(3)]
        off = [row8(recv_o[e, r : r + 1, :]) for r in range(3)]
        load = force + [
            off[1] * force[2] - off[2] * force[1],
            off[2] * force[0] - off[0] * force[2],
            off[0] * force[1] - off[1] * force[0],
        ]
        load = [jnp.where(mask, x, 0.0) for x in load]
        parts = [split2(x) for x in load]
        return jnp.concatenate([p[0] for p in parts] + [p[1] for p in parts], axis=0).astype(bf16)

    def arrival(k):
        return lax.rem(my_pair - k + pairs, pairs)

    def group_in(k, acc):
        g = arrival(k)
        block = recv_f.at[pl.ds(g * group, group)]
        pltpu.make_async_copy(block, block, sem_rf.at[g]).wait()
        for i in range(planes):
            p = g * planes + i
            left = jnp.concatenate([spread(2 * p), spread(2 * p + 1)], axis=1)
            acc = acc + lax.dot_general(
                left, hot[p], (((1,), (1,)), ((), ())), preferred_element_type=f32
            )
        return acc

    acc = lax.fori_loop(0, pairs, group_in, jnp.zeros((12 * HI, TILE), f32))

    tot_send[...] = acc[0 : 6 * HI, :] + acc[6 * HI : 12 * HI, :]
    swap_t = pltpu.make_async_remote_copy(
        src_ref=tot_send, dst_ref=tot_in, send_sem=sem_ps.at[1], recv_sem=sem_pr.at[1],
        device_id=(d, other), device_id_type=MESH,
    )
    swap_t.start()
    swap_t.wait()

    velocity = []
    for r in range(6):
        total = tot_send[r * HI : (r + 1) * HI, :] + tot_in[r * HI : (r + 1) * HI, :]
        value = cs8[r] + cs8[6 if r < 3 else 4 + r] * total
        if r == 2:
            value = value - gravity_step
        velocity.append(value)
        for h in range(HI):
            vel_out[r : r + 1, h * TILE : (h + 1) * TILE] = value[h : h + 1, :]
    parts = [split2(x) for x in velocity]
    vel8[...] = jnp.concatenate([p[0] for p in parts] + [p[1] for p in parts], axis=0).astype(bf16)

    def stage_v(p):
        got = jnp.dot(vel8[...], hot[p], preferred_element_type=f32)
        got = got[0 : 6 * HI] + got[6 * HI : 12 * HI]
        for half in range(2):
            e = 2 * p + half
            cols = slice(half * TILE, (half + 1) * TILE)
            high, _ = high_low(e)
            mask = row8(high) == high_rows
            mine = [got[r * HI : (r + 1) * HI, cols] for r in range(6)]
            off = [row8(recv_o[e, r : r + 1, :]) for r in range(3)]
            for r in range(3):
                r1, r2 = (r + 1) % 3, (r + 2) % 3
                value = mine[r] + mine[3 + r1] * off[r2] - mine[3 + r2] * off[r1]
                send_v[e, r : r + 1, :] = jnp.sum(
                    jnp.where(mask, value, 0.0), axis=0, keepdims=True
                )

    def stage_group(k):
        g = lax.rem(my_pair + k, pairs)
        for i in range(planes):
            stage_v(g * planes + i)

    def send_back(k, c):
        plane, pair, bit = peer(k)
        pltpu.make_async_remote_copy(
            src_ref=send_v.at[pair * group + plane * 2 + bit],
            dst_ref=recv_v.at[my_slot],
            send_sem=sem_sv,
            recv_sem=sem_rv.at[my_pair],
            device_id=(domain(plane, pair, bit), s),
            device_id_type=MESH,
        ).start()
        return c

    stage_group(0)
    lax.fori_loop(1, group, send_back, 0)
    pltpu.make_async_copy(send_v.at[my_slot], recv_v.at[my_slot], sem_rv.at[my_pair]).start()

    def push_v(k, c):
        stage_group(k)
        return lax.fori_loop(k * group, (k + 1) * group, send_back, c)

    lax.fori_loop(1, pairs, push_v, 0)

    def swap_v(g):
        block = pl.ds(g * group, group)
        return pltpu.make_async_remote_copy(
            src_ref=recv_v.at[block], dst_ref=part_v.at[block],
            send_sem=sem_vs, recv_sem=sem_vr.at[g],
            device_id=(d, other), device_id_type=MESH,
        )

    def write(parity, ref, g):
        for i in range(group):
            o = domain(i // 2, g, i % 2)
            first = pl.multiple_of((2 * o + parity) * TILE, TILE)
            sv_out[:, pl.ds(first, TILE)] = ref[g * group + i]

    def group_v(k, c):
        g = arrival(k)
        block = recv_v.at[pl.ds(g * group, group)]
        pltpu.make_async_copy(block, block, sem_rv.at[g]).wait()
        swap_v(g).start()
        write(s, recv_v, g)
        return c

    lax.fori_loop(0, pairs, group_v, 0)

    def group_p(k, c):
        g = arrival(k)
        block = part_v.at[pl.ds(g * group, group)]
        pltpu.make_async_copy(block, block, sem_vr.at[g]).wait()
        write(other, part_v, g)
        return c

    lax.fori_loop(0, pairs, group_p, 0)

    for ref, sem in ((send_o, sem_so), (send_f, sem_sf), (send_v, sem_sv)):
        block = ref.at[pl.ds(0, n - 1)]
        pltpu.make_async_copy(block, block, sem).wait()
    pltpu.make_async_copy(recv_v, recv_v, sem_vs).wait()


def stay(x):
    return pltpu.with_memory_space_constraint(x, pltpu.HBM)


def per_device(
    fluid_state,
    sphere_state,
    sphere_offset,
    tile_list,
    tile_count,
    clump_ids,
    clump_state,
    clump_inverse,
):
    n = lax.axis_size("space")
    slots = tile_list.shape[0]
    fluid_tiles = fluid_state.shape[1] // TILE
    spheres = sphere_state.shape[1]
    clumps = clump_state.shape[1]
    inner = 16 if n >= 32 else 4 if n >= 8 else 2
    pairs = inner // 2
    lists = tile_list.T
    vmem = pl.BlockSpec(memory_space=pltpu.VMEM)
    hbm = pl.BlockSpec(memory_space=pltpu.HBM)
    dma = pltpu.SemaphoreType.DMA
    block3 = pltpu.VMEM((n, 3, TILE), f32)
    block4 = pltpu.VMEM((n, 4, TILE), f32)
    planes = pltpu.VMEM((3, n, TILE), f32)
    return pl.pallas_call(
        functools.partial(kernel, n, slots, fluid_tiles, inner),
        out_shape=(
            jax.ShapeDtypeStruct((6, clumps), f32),
            jax.ShapeDtypeStruct((3, spheres), f32),
        ),
        in_specs=[hbm, pl.BlockSpec(memory_space=pltpu.SMEM)] + [hbm] * 6,
        out_specs=(vmem, vmem),
        scratch_shapes=[
            pltpu.SMEM((2, slots), jnp.int32),
            pltpu.VMEM((2, slots), jnp.int32),
            pltpu.VMEM(fluid_state.shape, f32),
            pltpu.VMEM(sphere_state.shape, f32),
            pltpu.VMEM(sphere_offset.shape, f32),
            pltpu.VMEM((spheres // TILE, TILE), jnp.int32),
            pltpu.VMEM(clump_state.shape, f32),
            pltpu.VMEM(clump_inverse.shape, f32),
            pltpu.VMEM((fluid_tiles, 3, TILE, TILE), f32),
            pltpu.VMEM((fluid_tiles, 64, TILE), bf16),
            pltpu.VMEM((2 * n, 7, TILE), f32),
            pltpu.VMEM((slots * 8, TILE), f32),
            planes,
            planes,
            planes,
            block4,
            block4,
            block3,
            block3,
            block3,
            block3,
            block3,
            pltpu.VMEM((n // 2, TILE, 2 * TILE), bf16),
            pltpu.VMEM((6 * HI, TILE), f32),
            pltpu.VMEM((6 * HI, TILE), f32),
            pltpu.VMEM((10, HI, TILE), f32),
            pltpu.VMEM((12 * HI, TILE), bf16),
            pltpu.SemaphoreType.REGULAR,
            dma((8,)),
            dma(()),
            dma(()),
            dma(()),
            dma((pairs,)),
            dma(()),
            dma((pairs,)),
            dma((2,)),
            dma((2,)),
            dma(()),
            dma((pairs,)),
        ],
        compiler_params=pltpu.CompilerParams(
            collective_id=0, has_side_effects=True, vmem_limit_bytes=40 << 20
        ),
        name="step",
    )(
        stay(lists),
        tile_count,
        stay(fluid_state),
        stay(sphere_state),
        stay(sphere_offset),
        stay(clump_ids.reshape(spheres // TILE, TILE)),
        stay(clump_state),
        stay(clump_inverse),
    )


def solution(mesh):
    in_specs = (
        P(None, "space"),
        P(None, "space"),
        P(None, "space"),
        P(("space", "sub"), None),
        P(("space", "sub")),
        P("space"),
        P(None, "space"),
        P(None, "space"),
    )
    out_specs = (P(None, "space"), P(None, "space"))
    return jax.shard_map(
        per_device, mesh=mesh, in_specs=in_specs, out_specs=out_specs, check_vma=False
    )
```

```python
import functools

import jax
import jax.numpy as jnp
from jax import lax
from jax.experimental import pallas as pl
from jax.experimental.pallas import tpu as pltpu
from jax.sharding import PartitionSpec as P

TILE = 128
SLOT_UNROLL = 16
PREP_UNROLL = 4
HI = 8

MESH = pl.DeviceIdType.MESH
f32 = jnp.float32
bf16 = jnp.bfloat16

press_coef = 4.0
gravity_step = 0.1


def split2(x):
    hi = x.astype(bf16).astype(f32)
    return hi, x - hi


def row8(row):
    return jnp.broadcast_to(row, (8, TILE))


def kernel(
    n,
    slots,
    fluid_tiles,
    inner,
    tl_h,
    cnt_s,
    fluid_h,
    sphere_h,
    offset_h,
    ids_h,
    cstate_h,
    cinv_h,
    vel_out,
    sv_out,
    tl_s,
    tl_v,
    fluid,
    sphere,
    offset,
    ids,
    cstate,
    cinv,
    fb,
    fcol,
    by_tile,
    terms,
    f_own,
    f_oth,
    f_in,
    send_o,
    recv_o,
    send_f,
    recv_f,
    send_v,
    recv_v,
    part_v,
    hot,
    tot_send,
    tot_in,
    cs8,
    vel8,
    sem_line,
    sem_in,
    sem_so,
    sem_ro,
    sem_sf,
    sem_rf,
    sem_sv,
    sem_rv,
    sem_ps,
    sem_pr,
    sem_vs,
    sem_vr,
):
    d = lax.axis_index("space")
    s = lax.axis_index("sub")
    other = 1 - s
    planes = n // inner
    pairs = inner // 2
    half_n = n // 2
    my_plane = d // inner
    my_pair = lax.rem(d, inner) // 2
    my_bit = lax.rem(d, 2)
    my_slot = my_pair * planes + my_plane
    to_self = my_bit == s
    turns = [
        lax.rem(my_plane + ((t + 1) // 2) * (1 - 2 * ((t + 1) % 2)) + planes, planes)
        for t in range(planes)
    ]

    def send_chunk(chunk, source, target, send_sem, recv_sem, by_slot):
        pair = lax.rem(my_pair + chunk, pairs)
        first = isinstance(chunk, int) and chunk == 0
        for t in range(planes):
            plane = turns[t]
            block = source.at[pair * planes + plane if by_slot else plane * pairs + pair]

            def remote():
                pltpu.make_async_remote_copy(
                    src_ref=block,
                    dst_ref=target.at[my_slot],
                    send_sem=send_sem,
                    recv_sem=recv_sem,
                    device_id=(plane * inner + 2 * pair + s, my_bit),
                    device_id_type=MESH,
                ).start()

            if first and t == 0:
                pl.when(jnp.logical_not(to_self))(remote)

                @pl.when(to_self)
                def _():
                    pltpu.make_async_copy(block, target.at[my_slot], recv_sem).start()
            else:
                remote()

    def send_all(source, target, send_sem, recv_sem):
        send_chunk(0, source, target, send_sem, recv_sem, False)

        def more(chunk, c):
            send_chunk(chunk, source, target, send_sem, recv_sem, False)
            return c

        lax.fori_loop(1, pairs, more, 0)

    loads = [
        pltpu.make_async_copy(src, dst, sem_in.at[i])
        for i, (src, dst) in enumerate(
            [
                (fluid_h, fluid),
                (sphere_h, sphere),
                (tl_h, tl_s),
                (offset_h, offset),
                (ids_h, ids),
                (tl_h, tl_v),
                (cstate_h, cstate),
                (cinv_h, cinv),
            ]
        )
    ]
    for copy in loads:
        copy.start()

    bar = pltpu.get_barrier_semaphore()

    def greet_plane(k, c):
        mate = my_plane * inner + 2 * lax.rem(my_pair + k, pairs) + s
        pl.semaphore_signal(bar, inc=1, device_id=(mate, my_bit), device_id_type=MESH)
        return c

    def line(k):
        return lax.rem(d + k * inner, n)

    def greet_line(k, c):
        pl.semaphore_signal(bar, inc=1, device_id=(line(k), s), device_id_type=MESH)
        return c

    def vouch(k, c):
        pl.semaphore_signal(sem_line, inc=1, device_id=(line(k), s), device_id_type=MESH)
        return c

    lax.fori_loop(1, planes, greet_line, 0)
    lax.fori_loop(1, pairs, greet_plane, 0)

    @pl.when(jnp.logical_not(to_self))
    def _():
        greet_plane(0, 0)

    pl.semaphore_signal(bar, inc=1, device_id=(d, other), device_id_type=MESH)

    loads[0].wait()

    def prep(b, c):
        tile = fluid[:, pl.ds(pl.multiple_of(b * TILE, TILE), TILE)]
        turned = jnp.transpose(tile * 2.0)
        for axis in range(3):
            fb[b, axis] = jnp.broadcast_to(turned[:, axis : axis + 1], (TILE, TILE))
        mass = tile[7:8]
        pm = tile[6:7] * mass
        centred = tile[0:3] - 0.5
        mx = mass * centred
        mv = mass * tile[3:6] - press_coef * (pm * centred)
        zero = jnp.zeros((5, TILE), f32)
        rows = jnp.concatenate(
            [
                jnp.broadcast_to(mass, (3, TILE)), zero,
                jnp.broadcast_to(pm, (3, TILE)), zero,
                mx, zero,
                mv, zero,
            ],
            axis=0,
        )
        hi, lo = split2(rows)
        fcol[b] = jnp.concatenate([hi, lo], axis=0).astype(bf16)
        return c

    lax.fori_loop(0, fluid_tiles, prep, 0, unroll=PREP_UNROLL)

    differ = my_bit + s - 2 * my_bit * s
    pl.semaphore_wait(bar, planes + pairs - 1 + differ)
    lax.fori_loop(1, planes, vouch, 0)

    loads[1].wait()

    def stage_s(a, c):
        by_tile[a] = sphere[:, pl.ds(pl.multiple_of(a * TILE, TILE), TILE)]
        return c

    lax.fori_loop(0, 2 * n, stage_s, 0, unroll=8)

    loads[3].wait()
    loads[4].wait()

    def stage_o(i, c):
        for half in range(2):
            tile = 4 * i + 2 * s + half
            send_o[i, half, 0:3, :] = offset[:, pl.ds(pl.multiple_of(tile * TILE, TILE), TILE)]
            send_o[i, half, 3:4, :] = ids[pl.ds(tile, 1), :].astype(f32)
        return c

    lax.fori_loop(0, half_n, stage_o, 0, unroll=min(half_n, 4))

    for i in (2, 5, 6, 7):
        loads[i].wait()

    pl.semaphore_wait(sem_line, planes - 1)

    send_all(send_o, recv_o, sem_so, sem_ro)

    def slot(t, c):
        a = tl_s[0, t]
        b = tl_s[1, t]
        spheres = by_tile[a]
        twice = spheres[0:3] * 2.0
        sep = twice[0:1] - fb[b, 0]
        d2 = sep * sep
        sep = twice[1:2] - fb[b, 1]
        d2 = d2 + sep * sep
        sep = twice[2:3] - fb[b, 2]
        d2 = d2 + sep * sep
        d2 = jnp.maximum(d2, 1e-30)
        fall = jnp.maximum(1.0 - d2 * lax.rsqrt(d2), 0.0)
        cube = fall * fall * fall
        hi = cube.astype(bf16)
        lo = (cube - hi.astype(f32)).astype(bf16)
        col = fcol[b]
        sums = jnp.dot(
            jnp.concatenate([col, col], axis=1),
            jnp.concatenate([hi, lo], axis=0),
            preferred_element_type=f32,
        )
        sums = sums[0:32] + sums[32:64]
        x3 = spheres[0:3] - 0.5
        p4 = press_coef * spheres[6:7]
        force = (
            sums[0:3] * (p4 * x3 - spheres[3:6])
            + (press_coef * x3) * sums[8:11]
            - p4 * sums[16:19]
            + sums[24:27]
        )
        terms[pl.ds(pl.multiple_of(t * 8, 8), 3), :] = force
        return c

    lax.fori_loop(0, slots, slot, 0, unroll=min(slots, SLOT_UNROLL))

    lists = tl_v[0:1, :]
    live = lax.broadcasted_iota(jnp.int32, (n, slots), 1) < cnt_s[0]
    row = lax.broadcasted_iota(jnp.int32, (n, slots), 0)
    tile_row = jnp.where(row < half_n, 4 * row, 4 * (row - half_n) + 1)

    def place(parity, out):
        match = jnp.where(
            live & (jnp.broadcast_to(lists, (n, slots)) == tile_row + 2 * parity), 1.0, 0.0
        ).astype(bf16)
        for axis in range(3):
            rows = terms[pl.ds(axis, slots, stride=8), :]
            hi, lo = split2(rows)
            out[axis] = jnp.dot(match, hi.astype(bf16), preferred_element_type=f32) + jnp.dot(
                match, lo.astype(bf16), preferred_element_type=f32
            )

    place(other, f_oth)
    swap_f = pltpu.make_async_remote_copy(
        src_ref=f_oth, dst_ref=f_in, send_sem=sem_ps.at[0], recv_sem=sem_pr.at[0],
        device_id=(d, other), device_id_type=MESH,
    )
    swap_f.start()
    place(s, f_own)
    swap_f.wait()

    def stage_f(i, c):
        for half in range(2):
            at = pl.ds(half * half_n + i, 1)
            for axis in range(3):
                send_f[i, half, axis : axis + 1, :] = f_own[axis, at, :] + f_in[axis, at, :]
        return c

    lax.fori_loop(0, half_n, stage_f, 0, unroll=min(half_n, 8))

    send_all(send_f, recv_f, sem_sf, sem_rf.at[my_pair])

    for r in range(6):
        for h in range(HI):
            cs8[r, h : h + 1, :] = cstate[r : r + 1, h * TILE : (h + 1) * TILE]
    for r in range(4):
        for h in range(HI):
            cs8[6 + r, h : h + 1, :] = cinv[r : r + 1, h * TILE : (h + 1) * TILE]

    pltpu.make_async_copy(recv_o, recv_o, sem_ro).wait()
    low_rows = lax.broadcasted_iota(jnp.int32, (TILE, TILE), 0).astype(f32)
    high_rows = lax.broadcasted_iota(jnp.int32, (HI, TILE), 0).astype(f32)

    def high_low(e, half):
        label = recv_o[e, half, 3:4, :]
        high = jnp.floor(label * (1.0 / TILE))
        return high, label - high * TILE

    def build(e, c):
        pieces = []
        for half in range(2):
            _, low = high_low(e, half)
            pieces.append(
                jnp.where(jnp.broadcast_to(low, (TILE, TILE)) == low_rows, 1.0, 0.0).astype(bf16)
            )
        hot[e] = jnp.concatenate(pieces, axis=1)
        return c

    lax.fori_loop(0, half_n, build, 0, unroll=2)

    def spread(e, half):
        high, _ = high_low(e, half)
        mask = row8(high) == high_rows
        force = [row8(recv_f[e, half, r : r + 1, :]) for r in range(3)]
        off = [row8(recv_o[e, half, r : r + 1, :]) for r in range(3)]
        load = force + [
            off[1] * force[2] - off[2] * force[1],
            off[2] * force[0] - off[0] * force[2],
            off[0] * force[1] - off[1] * force[0],
        ]
        load = [jnp.where(mask, x, 0.0) for x in load]
        parts = [split2(x) for x in load]
        return jnp.concatenate([p[0] for p in parts] + [p[1] for p in parts], axis=0).astype(bf16)

    def arrival(k):
        return lax.rem(my_pair - k + pairs, pairs)

    def group_in(k, acc):
        g = arrival(k)
        block = recv_f.at[pl.ds(g * planes, planes)]
        pltpu.make_async_copy(block, block, sem_rf.at[g]).wait()
        for i in range(planes):
            e = g * planes + i
            left = jnp.concatenate([spread(e, 0), spread(e, 1)], axis=1)
            acc = acc + lax.dot_general(
                left, hot[e], (((1,), (1,)), ((), ())), preferred_element_type=f32
            )
        return acc

    acc = lax.fori_loop(0, pairs, group_in, jnp.zeros((12 * HI, TILE), f32))

    tot_send[...] = acc[0 : 6 * HI, :] + acc[6 * HI : 12 * HI, :]
    swap_t = pltpu.make_async_remote_copy(
        src_ref=tot_send, dst_ref=tot_in, send_sem=sem_ps.at[1], recv_sem=sem_pr.at[1],
        device_id=(d, other), device_id_type=MESH,
    )
    swap_t.start()
    swap_t.wait()

    velocity = []
    for r in range(6):
        total = tot_send[r * HI : (r + 1) * HI, :] + tot_in[r * HI : (r + 1) * HI, :]
        value = cs8[r] + cs8[6 if r < 3 else 4 + r] * total
        if r == 2:
            value = value - gravity_step
        velocity.append(value)
        for h in range(HI):
            vel_out[r : r + 1, h * TILE : (h + 1) * TILE] = value[h : h + 1, :]
    parts = [split2(x) for x in velocity]
    vel8[...] = jnp.concatenate([p[0] for p in parts] + [p[1] for p in parts], axis=0).astype(bf16)

    def stage_v(e):
        got = jnp.dot(vel8[...], hot[e], preferred_element_type=f32)
        got = got[0 : 6 * HI] + got[6 * HI : 12 * HI]
        for half in range(2):
            cols = slice(half * TILE, (half + 1) * TILE)
            high, _ = high_low(e, half)
            mask = row8(high) == high_rows
            mine = [got[r * HI : (r + 1) * HI, cols] for r in range(6)]
            off = [row8(recv_o[e, half, r : r + 1, :]) for r in range(3)]
            for r in range(3):
                r1, r2 = (r + 1) % 3, (r + 2) % 3
                value = mine[r] + mine[3 + r1] * off[r2] - mine[3 + r2] * off[r1]
                send_v[e, half, r : r + 1, :] = jnp.sum(
                    jnp.where(mask, value, 0.0), axis=0, keepdims=True
                )

    def push_v(chunk, c):
        g = lax.rem(my_pair + chunk, pairs)
        for i in range(planes):
            stage_v(g * planes + i)
        send_chunk(chunk, send_v, recv_v, sem_sv, sem_rv.at[my_pair], True)
        return c

    push_v(0, 0)
    lax.fori_loop(1, pairs, push_v, 0)

    def swap_v(g):
        block = pl.ds(g * planes, planes)
        return pltpu.make_async_remote_copy(
            src_ref=recv_v.at[block], dst_ref=part_v.at[block],
            send_sem=sem_vs, recv_sem=sem_vr.at[g],
            device_id=(d, other), device_id_type=MESH,
        )

    def write(parity, ref, g):
        for plane in range(planes):
            owner = plane * inner + 2 * g + parity
            for half in range(2):
                first = pl.multiple_of((2 * owner + half) * TILE, TILE)
                sv_out[:, pl.ds(first, TILE)] = ref[g * planes + plane, half]

    def group_v(k, c):
        g = arrival(k)
        block = recv_v.at[pl.ds(g * planes, planes)]
        pltpu.make_async_copy(block, block, sem_rv.at[g]).wait()
        swap_v(g).start()
        write(s, recv_v, g)
        return c

    lax.fori_loop(0, pairs, group_v, 0)

    def group_p(k, c):
        g = arrival(k)
        block = part_v.at[pl.ds(g * planes, planes)]
        pltpu.make_async_copy(block, block, sem_vr.at[g]).wait()
        write(other, part_v, g)
        return c

    lax.fori_loop(0, pairs, group_p, 0)

    for ref, sem in ((send_o, sem_so), (send_f, sem_sf), (send_v, sem_sv)):
        block = ref.at[pl.ds(0, half_n - 1)]
        pltpu.make_async_copy(block, block, sem).wait()

    @pl.when(jnp.logical_not(to_self))
    def _():
        for ref, sem in ((send_o, sem_so), (send_f, sem_sf), (send_v, sem_sv)):
            pltpu.make_async_copy(ref.at[0], ref.at[0], sem).wait()

    pltpu.make_async_copy(recv_v, recv_v, sem_vs).wait()


def stay(x):
    return pltpu.with_memory_space_constraint(x, pltpu.HBM)


def per_device(
    fluid_state,
    sphere_state,
    sphere_offset,
    tile_list,
    tile_count,
    clump_ids,
    clump_state,
    clump_inverse,
):
    n = lax.axis_size("space")
    slots = tile_list.shape[0]
    fluid_tiles = fluid_state.shape[1] // TILE
    spheres = sphere_state.shape[1]
    clumps = clump_state.shape[1]
    inner = 16 if n >= 32 else 4 if n >= 8 else 2
    pairs = inner // 2
    lists = tile_list.T
    vmem = pl.BlockSpec(memory_space=pltpu.VMEM)
    hbm = pl.BlockSpec(memory_space=pltpu.HBM)
    dma = pltpu.SemaphoreType.DMA
    block3 = pltpu.VMEM((n // 2, 2, 3, TILE), f32)
    block4 = pltpu.VMEM((n // 2, 2, 4, TILE), f32)
    planes = pltpu.VMEM((3, n, TILE), f32)
    return pl.pallas_call(
        functools.partial(kernel, n, slots, fluid_tiles, inner),
        out_shape=(
            jax.ShapeDtypeStruct((6, clumps), f32),
            jax.ShapeDtypeStruct((3, spheres), f32),
        ),
        in_specs=[hbm, pl.BlockSpec(memory_space=pltpu.SMEM)] + [hbm] * 6,
        out_specs=(vmem, vmem),
        scratch_shapes=[
            pltpu.SMEM((2, slots), jnp.int32),
            pltpu.VMEM((2, slots), jnp.int32),
            pltpu.VMEM(fluid_state.shape, f32),
            pltpu.VMEM(sphere_state.shape, f32),
            pltpu.VMEM(sphere_offset.shape, f32),
            pltpu.VMEM((spheres // TILE, TILE), jnp.int32),
            pltpu.VMEM(clump_state.shape, f32),
            pltpu.VMEM(clump_inverse.shape, f32),
            pltpu.VMEM((fluid_tiles, 3, TILE, TILE), f32),
            pltpu.VMEM((fluid_tiles, 64, TILE), bf16),
            pltpu.VMEM((2 * n, 7, TILE), f32),
            pltpu.VMEM((slots * 8, TILE), f32),
            planes,
            planes,
            planes,
            block4,
            block4,
            block3,
            block3,
            block3,
            block3,
            block3,
            pltpu.VMEM((n // 2, TILE, 2 * TILE), bf16),
            pltpu.VMEM((6 * HI, TILE), f32),
            pltpu.VMEM((6 * HI, TILE), f32),
            pltpu.VMEM((10, HI, TILE), f32),
            pltpu.VMEM((12 * HI, TILE), bf16),
            pltpu.SemaphoreType.REGULAR,
            dma((8,)),
            dma(()),
            dma(()),
            dma(()),
            dma((pairs,)),
            dma(()),
            dma((pairs,)),
            dma((2,)),
            dma((2,)),
            dma(()),
            dma((pairs,)),
        ],
        compiler_params=pltpu.CompilerParams(
            collective_id=0, has_side_effects=True, vmem_limit_bytes=40 << 20
        ),
        name="step",
    )(
        stay(lists),
        tile_count,
        stay(fluid_state),
        stay(sphere_state),
        stay(sphere_offset),
        stay(clump_ids.reshape(spheres // TILE, TILE)),
        stay(clump_state),
        stay(clump_inverse),
    )


def solution(mesh):
    in_specs = (
        P(None, "space"),
        P(None, "space"),
        P(None, "space"),
        P(("space", "sub"), None),
        P(("space", "sub")),
        P("space"),
        P(None, "space"),
        P(None, "space"),
    )
    out_specs = (P(None, "space"), P(None, "space"))
    return jax.shard_map(
        per_device, mesh=mesh, in_specs=in_specs, out_specs=out_specs, check_vma=False
    )
```

```python
import functools

import jax
import jax.numpy as jnp
from jax import lax
from jax.experimental import pallas as pl
from jax.experimental.pallas import tpu as pltpu
from jax.sharding import PartitionSpec as P

TILE = 128
SLOT_UNROLL = 16
PREP_UNROLL = 4
HI = 8

MESH = pl.DeviceIdType.MESH
f32 = jnp.float32
bf16 = jnp.bfloat16

press_coef = 4.0
gravity_step = 0.1


def split2(x):
    hi = x.astype(bf16).astype(f32)
    return hi, x - hi


def row8(row):
    return jnp.broadcast_to(row, (8, TILE))


def kernel(
    n,
    slots,
    fluid_tiles,
    inner,
    tl_h,
    cnt_s,
    fluid_h,
    sphere_h,
    offset_h,
    ids_h,
    cstate_h,
    cinv_h,
    vel_out,
    sv_out,
    tl_s,
    tl_v,
    fluid,
    sphere,
    offset,
    ids,
    cstate,
    cinv,
    fb,
    fcol,
    by_tile,
    terms,
    f_own,
    f_oth,
    f_in,
    send_o,
    recv_o,
    send_f,
    recv_f,
    send_v,
    recv_v,
    part_v,
    hot,
    tot_send,
    tot_in,
    cs8,
    vel8,
    sem_in,
    sem_so,
    sem_ro,
    sem_sf,
    sem_rf,
    sem_sv,
    sem_rv,
    sem_ps,
    sem_pr,
    sem_vs,
    sem_vr,
):
    d = lax.axis_index("space")
    s = lax.axis_index("sub")
    other = 1 - s
    planes = n // inner
    pairs = inner // 2
    half_n = n // 2
    my_plane = d // inner
    my_pair = lax.rem(d, inner) // 2
    my_bit = lax.rem(d, 2)
    my_slot = my_pair * planes + my_plane
    to_self = my_bit == s
    turns = [
        lax.rem(my_plane + ((t + 1) // 2) * (1 - 2 * ((t + 1) % 2)) + planes, planes)
        for t in range(planes)
    ]

    def send_chunk(chunk, source, target, send_sem, recv_sem, by_slot):
        pair = lax.rem(my_pair + chunk, pairs)
        first = isinstance(chunk, int) and chunk == 0
        for t in range(planes):
            plane = turns[t]
            block = source.at[pair * planes + plane if by_slot else plane * pairs + pair]

            def remote():
                pltpu.make_async_remote_copy(
                    src_ref=block,
                    dst_ref=target.at[my_slot],
                    send_sem=send_sem,
                    recv_sem=recv_sem,
                    device_id=(plane * inner + 2 * pair + s, my_bit),
                    device_id_type=MESH,
                ).start()

            if first and t == 0:
                pl.when(jnp.logical_not(to_self))(remote)

                @pl.when(to_self)
                def _():
                    pltpu.make_async_copy(block, target.at[my_slot], recv_sem).start()
            else:
                remote()

    def send_all(source, target, send_sem, recv_sem):
        send_chunk(0, source, target, send_sem, recv_sem, False)

        def more(chunk, c):
            send_chunk(chunk, source, target, send_sem, recv_sem, False)
            return c

        lax.fori_loop(1, pairs, more, 0)

    loads = [
        pltpu.make_async_copy(src, dst, sem_in.at[i])
        for i, (src, dst) in enumerate(
            [
                (offset_h, offset),
                (ids_h, ids),
                (fluid_h, fluid),
                (sphere_h, sphere),
                (tl_h, tl_s),
                (tl_h, tl_v),
                (cstate_h, cstate),
                (cinv_h, cinv),
            ]
        )
    ]
    for copy in loads:
        copy.start()

    bar = pltpu.get_barrier_semaphore()

    def greet(plane, pair):
        mate = plane * inner + 2 * pair + s
        pl.semaphore_signal(bar, inc=1, device_id=(mate, my_bit), device_id_type=MESH)

    def greet_chunk(chunk, c):
        pair = lax.rem(my_pair + chunk, pairs)
        for t in range(planes):
            greet(turns[t], pair)
        return c

    for t in range(1, planes):
        greet(turns[t], my_pair)
    lax.fori_loop(1, pairs, greet_chunk, 0)

    @pl.when(jnp.logical_not(to_self))
    def _():
        greet(my_plane, my_pair)

    pl.semaphore_signal(bar, inc=1, device_id=(d, other), device_id_type=MESH)

    loads[0].wait()
    loads[1].wait()

    def stage_o(i, c):
        for half in range(2):
            tile = 4 * i + 2 * s + half
            send_o[i, half, 0:3, :] = offset[:, pl.ds(pl.multiple_of(tile * TILE, TILE), TILE)]
            send_o[i, half, 3:4, :] = ids[pl.ds(tile, 1), :].astype(f32)
        return c

    lax.fori_loop(0, half_n, stage_o, 0, unroll=min(half_n, 4))

    differ = my_bit + s - 2 * my_bit * s
    pl.semaphore_wait(bar, half_n + differ)

    send_all(send_o, recv_o, sem_so, sem_ro)

    loads[2].wait()

    def prep(b, c):
        tile = fluid[:, pl.ds(pl.multiple_of(b * TILE, TILE), TILE)]
        turned = jnp.transpose(tile * 2.0)
        for axis in range(3):
            fb[b, axis] = jnp.broadcast_to(turned[:, axis : axis + 1], (TILE, TILE))
        mass = tile[7:8]
        pm = tile[6:7] * mass
        centred = tile[0:3] - 0.5
        mx = mass * centred
        mv = mass * tile[3:6] - press_coef * (pm * centred)
        zero = jnp.zeros((5, TILE), f32)
        rows = jnp.concatenate(
            [
                jnp.broadcast_to(mass, (3, TILE)), zero,
                jnp.broadcast_to(pm, (3, TILE)), zero,
                mx, zero,
                mv, zero,
            ],
            axis=0,
        )
        hi, lo = split2(rows)
        fcol[b] = jnp.concatenate([hi, lo], axis=0).astype(bf16)
        return c

    lax.fori_loop(0, fluid_tiles, prep, 0, unroll=PREP_UNROLL)

    loads[3].wait()

    def stage_s(a, c):
        by_tile[a] = sphere[:, pl.ds(pl.multiple_of(a * TILE, TILE), TILE)]
        return c

    lax.fori_loop(0, 2 * n, stage_s, 0, unroll=8)

    for i in (4, 5, 6, 7):
        loads[i].wait()

    def slot(t, c):
        a = tl_s[0, t]
        b = tl_s[1, t]
        spheres = by_tile[a]
        twice = spheres[0:3] * 2.0
        sep = twice[0:1] - fb[b, 0]
        d2 = sep * sep
        sep = twice[1:2] - fb[b, 1]
        d2 = d2 + sep * sep
        sep = twice[2:3] - fb[b, 2]
        d2 = d2 + sep * sep
        d2 = jnp.maximum(d2, 1e-30)
        fall = jnp.maximum(1.0 - d2 * lax.rsqrt(d2), 0.0)
        cube = fall * fall * fall
        hi = cube.astype(bf16)
        lo = (cube - hi.astype(f32)).astype(bf16)
        col = fcol[b]
        sums = jnp.dot(
            jnp.concatenate([col, col], axis=1),
            jnp.concatenate([hi, lo], axis=0),
            preferred_element_type=f32,
        )
        sums = sums[0:32] + sums[32:64]
        x3 = spheres[0:3] - 0.5
        p4 = press_coef * spheres[6:7]
        force = (
            sums[0:3] * (p4 * x3 - spheres[3:6])
            + (press_coef * x3) * sums[8:11]
            - p4 * sums[16:19]
            + sums[24:27]
        )
        terms[pl.ds(pl.multiple_of(t * 8, 8), 3), :] = force
        return c

    lax.fori_loop(0, slots, slot, 0, unroll=min(slots, SLOT_UNROLL))

    lists = tl_v[0:1, :]
    live = lax.broadcasted_iota(jnp.int32, (n, slots), 1) < cnt_s[0]
    row = lax.broadcasted_iota(jnp.int32, (n, slots), 0)
    tile_row = jnp.where(row < half_n, 4 * row, 4 * (row - half_n) + 1)

    def place(parity, out):
        match = jnp.where(
            live & (jnp.broadcast_to(lists, (n, slots)) == tile_row + 2 * parity), 1.0, 0.0
        ).astype(bf16)
        for axis in range(3):
            rows = terms[pl.ds(axis, slots, stride=8), :]
            hi, lo = split2(rows)
            out[axis] = jnp.dot(match, hi.astype(bf16), preferred_element_type=f32) + jnp.dot(
                match, lo.astype(bf16), preferred_element_type=f32
            )

    place(other, f_oth)
    swap_f = pltpu.make_async_remote_copy(
        src_ref=f_oth, dst_ref=f_in, send_sem=sem_ps.at[0], recv_sem=sem_pr.at[0],
        device_id=(d, other), device_id_type=MESH,
    )
    swap_f.start()
    place(s, f_own)
    swap_f.wait()

    def stage_f(i, c):
        for half in range(2):
            at = pl.ds(half * half_n + i, 1)
            for axis in range(3):
                send_f[i, half, axis : axis + 1, :] = f_own[axis, at, :] + f_in[axis, at, :]
        return c

    lax.fori_loop(0, half_n, stage_f, 0, unroll=min(half_n, 8))

    send_all(send_f, recv_f, sem_sf, sem_rf.at[my_pair])

    for r in range(6):
        for h in range(HI):
            cs8[r, h : h + 1, :] = cstate[r : r + 1, h * TILE : (h + 1) * TILE]
    for r in range(4):
        for h in range(HI):
            cs8[6 + r, h : h + 1, :] = cinv[r : r + 1, h * TILE : (h + 1) * TILE]

    pltpu.make_async_copy(recv_o, recv_o, sem_ro).wait()
    low_rows = lax.broadcasted_iota(jnp.int32, (TILE, TILE), 0).astype(f32)
    high_rows = lax.broadcasted_iota(jnp.int32, (HI, TILE), 0).astype(f32)

    def high_low(e, half):
        label = recv_o[e, half, 3:4, :]
        high = jnp.floor(label * (1.0 / TILE))
        return high, label - high * TILE

    def build(e, c):
        pieces = []
        for half in range(2):
            _, low = high_low(e, half)
            pieces.append(
                jnp.where(jnp.broadcast_to(low, (TILE, TILE)) == low_rows, 1.0, 0.0).astype(bf16)
            )
        hot[e] = jnp.concatenate(pieces, axis=1)
        return c

    lax.fori_loop(0, half_n, build, 0, unroll=2)

    def spread(e, half):
        high, _ = high_low(e, half)
        mask = row8(high) == high_rows
        force = [row8(recv_f[e, half, r : r + 1, :]) for r in range(3)]
        off = [row8(recv_o[e, half, r : r + 1, :]) for r in range(3)]
        load = force + [
            off[1] * force[2] - off[2] * force[1],
            off[2] * force[0] - off[0] * force[2],
            off[0] * force[1] - off[1] * force[0],
        ]
        load = [jnp.where(mask, x, 0.0) for x in load]
        parts = [split2(x) for x in load]
        return jnp.concatenate([p[0] for p in parts] + [p[1] for p in parts], axis=0).astype(bf16)

    def arrival(k):
        return lax.rem(my_pair - k + pairs, pairs)

    def group_in(k, acc):
        g = arrival(k)
        block = recv_f.at[pl.ds(g * planes, planes)]
        pltpu.make_async_copy(block, block, sem_rf.at[g]).wait()
        for i in range(planes):
            e = g * planes + i
            left = jnp.concatenate([spread(e, 0), spread(e, 1)], axis=1)
            acc = acc + lax.dot_general(
                left, hot[e], (((1,), (1,)), ((), ())), preferred_element_type=f32
            )
        return acc

    acc = lax.fori_loop(0, pairs, group_in, jnp.zeros((12 * HI, TILE), f32))

    tot_send[...] = acc[0 : 6 * HI, :] + acc[6 * HI : 12 * HI, :]
    swap_t = pltpu.make_async_remote_copy(
        src_ref=tot_send, dst_ref=tot_in, send_sem=sem_ps.at[1], recv_sem=sem_pr.at[1],
        device_id=(d, other), device_id_type=MESH,
    )
    swap_t.start()
    swap_t.wait()

    velocity = []
    for r in range(6):
        total = tot_send[r * HI : (r + 1) * HI, :] + tot_in[r * HI : (r + 1) * HI, :]
        value = cs8[r] + cs8[6 if r < 3 else 4 + r] * total
        if r == 2:
            value = value - gravity_step
        velocity.append(value)
        for h in range(HI):
            vel_out[r : r + 1, h * TILE : (h + 1) * TILE] = value[h : h + 1, :]
    parts = [split2(x) for x in velocity]
    vel8[...] = jnp.concatenate([p[0] for p in parts] + [p[1] for p in parts], axis=0).astype(bf16)

    def stage_v(e):
        got = jnp.dot(vel8[...], hot[e], preferred_element_type=f32)
        got = got[0 : 6 * HI] + got[6 * HI : 12 * HI]
        for half in range(2):
            cols = slice(half * TILE, (half + 1) * TILE)
            high, _ = high_low(e, half)
            mask = row8(high) == high_rows
            mine = [got[r * HI : (r + 1) * HI, cols] for r in range(6)]
            off = [row8(recv_o[e, half, r : r + 1, :]) for r in range(3)]
            for r in range(3):
                r1, r2 = (r + 1) % 3, (r + 2) % 3
                value = mine[r] + mine[3 + r1] * off[r2] - mine[3 + r2] * off[r1]
                send_v[e, half, r : r + 1, :] = jnp.sum(
                    jnp.where(mask, value, 0.0), axis=0, keepdims=True
                )

    def push_v(chunk, c):
        g = lax.rem(my_pair + chunk, pairs)
        for i in range(planes):
            stage_v(g * planes + i)
        send_chunk(chunk, send_v, recv_v, sem_sv, sem_rv.at[my_pair], True)
        return c

    push_v(0, 0)
    lax.fori_loop(1, pairs, push_v, 0)

    def swap_v(g):
        block = pl.ds(g * planes, planes)
        return pltpu.make_async_remote_copy(
            src_ref=recv_v.at[block], dst_ref=part_v.at[block],
            send_sem=sem_vs, recv_sem=sem_vr.at[g],
            device_id=(d, other), device_id_type=MESH,
        )

    def write(parity, ref, g):
        for plane in range(planes):
            owner = plane * inner + 2 * g + parity
            for half in range(2):
                first = pl.multiple_of((2 * owner + half) * TILE, TILE)
                sv_out[:, pl.ds(first, TILE)] = ref[g * planes + plane, half]

    def group_v(k, c):
        g = arrival(k)
        block = recv_v.at[pl.ds(g * planes, planes)]
        pltpu.make_async_copy(block, block, sem_rv.at[g]).wait()
        swap_v(g).start()
        write(s, recv_v, g)
        return c

    lax.fori_loop(0, pairs, group_v, 0)

    def group_p(k, c):
        g = arrival(k)
        block = part_v.at[pl.ds(g * planes, planes)]
        pltpu.make_async_copy(block, block, sem_vr.at[g]).wait()
        write(other, part_v, g)
        return c

    lax.fori_loop(0, pairs, group_p, 0)

    for ref, sem in ((send_o, sem_so), (send_f, sem_sf), (send_v, sem_sv)):
        block = ref.at[pl.ds(0, half_n - 1)]
        pltpu.make_async_copy(block, block, sem).wait()

    @pl.when(jnp.logical_not(to_self))
    def _():
        for ref, sem in ((send_o, sem_so), (send_f, sem_sf), (send_v, sem_sv)):
            pltpu.make_async_copy(ref.at[0], ref.at[0], sem).wait()

    pltpu.make_async_copy(recv_v, recv_v, sem_vs).wait()


def stay(x):
    return pltpu.with_memory_space_constraint(x, pltpu.HBM)


def per_device(
    fluid_state,
    sphere_state,
    sphere_offset,
    tile_list,
    tile_count,
    clump_ids,
    clump_state,
    clump_inverse,
):
    n = lax.axis_size("space")
    slots = tile_list.shape[0]
    fluid_tiles = fluid_state.shape[1] // TILE
    spheres = sphere_state.shape[1]
    clumps = clump_state.shape[1]
    inner = 16 if n >= 32 else 4 if n >= 8 else 2
    pairs = inner // 2
    lists = tile_list.T
    vmem = pl.BlockSpec(memory_space=pltpu.VMEM)
    hbm = pl.BlockSpec(memory_space=pltpu.HBM)
    dma = pltpu.SemaphoreType.DMA
    block3 = pltpu.VMEM((n // 2, 2, 3, TILE), f32)
    block4 = pltpu.VMEM((n // 2, 2, 4, TILE), f32)
    planes = pltpu.VMEM((3, n, TILE), f32)
    return pl.pallas_call(
        functools.partial(kernel, n, slots, fluid_tiles, inner),
        out_shape=(
            jax.ShapeDtypeStruct((6, clumps), f32),
            jax.ShapeDtypeStruct((3, spheres), f32),
        ),
        in_specs=[hbm, pl.BlockSpec(memory_space=pltpu.SMEM)] + [hbm] * 6,
        out_specs=(vmem, vmem),
        scratch_shapes=[
            pltpu.SMEM((2, slots), jnp.int32),
            pltpu.VMEM((2, slots), jnp.int32),
            pltpu.VMEM(fluid_state.shape, f32),
            pltpu.VMEM(sphere_state.shape, f32),
            pltpu.VMEM(sphere_offset.shape, f32),
            pltpu.VMEM((spheres // TILE, TILE), jnp.int32),
            pltpu.VMEM(clump_state.shape, f32),
            pltpu.VMEM(clump_inverse.shape, f32),
            pltpu.VMEM((fluid_tiles, 3, TILE, TILE), f32),
            pltpu.VMEM((fluid_tiles, 64, TILE), bf16),
            pltpu.VMEM((2 * n, 7, TILE), f32),
            pltpu.VMEM((slots * 8, TILE), f32),
            planes,
            planes,
            planes,
            block4,
            block4,
            block3,
            block3,
            block3,
            block3,
            block3,
            pltpu.VMEM((n // 2, TILE, 2 * TILE), bf16),
            pltpu.VMEM((6 * HI, TILE), f32),
            pltpu.VMEM((6 * HI, TILE), f32),
            pltpu.VMEM((10, HI, TILE), f32),
            pltpu.VMEM((12 * HI, TILE), bf16),
            dma((8,)),
            dma(()),
            dma(()),
            dma(()),
            dma((pairs,)),
            dma(()),
            dma((pairs,)),
            dma((2,)),
            dma((2,)),
            dma(()),
            dma((pairs,)),
        ],
        compiler_params=pltpu.CompilerParams(
            collective_id=0, has_side_effects=True, vmem_limit_bytes=40 << 20
        ),
        name="step",
    )(
        stay(lists),
        tile_count,
        stay(fluid_state),
        stay(sphere_state),
        stay(sphere_offset),
        stay(clump_ids.reshape(spheres // TILE, TILE)),
        stay(clump_state),
        stay(clump_inverse),
    )


def solution(mesh):
    in_specs = (
        P(None, "space"),
        P(None, "space"),
        P(None, "space"),
        P(("space", "sub"), None),
        P(("space", "sub")),
        P("space"),
        P(None, "space"),
        P(None, "space"),
    )
    out_specs = (P(None, "space"), P(None, "space"))
    return jax.shard_map(
        per_device, mesh=mesh, in_specs=in_specs, out_specs=out_specs, check_vma=False
    )
```

```python
import functools

import jax
import jax.numpy as jnp
from jax import lax
from jax.experimental import pallas as pl
from jax.experimental.pallas import tpu as pltpu
from jax.sharding import PartitionSpec as P

TILE = 128
SLOT_UNROLL = 32
PREP_UNROLL = 4
HI = 8

MESH = pl.DeviceIdType.MESH
f32 = jnp.float32
bf16 = jnp.bfloat16

press_coef = 4.0
gravity_step = 0.1


def split2(x):
    hi = x.astype(bf16).astype(f32)
    return hi, x - hi


def row8(row):
    return jnp.broadcast_to(row, (8, TILE))


def kernel(
    n,
    slots,
    fluid_tiles,
    inner,
    tl_h,
    cnt_s,
    fluid_h,
    sphere_h,
    offset_h,
    ids_h,
    cstate_h,
    cinv_h,
    vel_out,
    sv_out,
    tl_s,
    tl_v,
    fluid,
    sphere,
    offset,
    ids,
    cstate,
    cinv,
    fb,
    fcol,
    by_tile,
    terms,
    f_own,
    f_oth,
    f_in,
    send_o,
    recv_o,
    send_f,
    recv_f,
    send_v,
    recv_v,
    part_v,
    hot,
    tot_send,
    tot_in,
    cs8,
    vel8,
    sem_in,
    sem_so,
    sem_ro,
    sem_sf,
    sem_rf,
    sem_sv,
    sem_rv,
    sem_ps,
    sem_pr,
    sem_vs,
    sem_vr,
):
    d = lax.axis_index("space")
    s = lax.axis_index("sub")
    other = 1 - s
    planes = n // inner
    pairs = inner // 2
    half_n = n // 2
    my_plane = d // inner
    my_pair = lax.rem(d, inner) // 2
    my_bit = lax.rem(d, 2)
    my_slot = my_pair * planes + my_plane
    to_self = my_bit == s
    turns = [
        lax.rem(my_plane + ((t + 1) // 2) * (1 - 2 * ((t + 1) % 2)) + planes, planes)
        for t in range(planes)
    ]

    def send_chunk(chunk, source, target, send_sem, recv_sem, by_slot):
        pair = lax.rem(my_pair + chunk, pairs)
        first = isinstance(chunk, int) and chunk == 0
        for t in reversed(range(planes)):
            plane = turns[t]
            block = source.at[pair * planes + plane if by_slot else plane * pairs + pair]

            def remote():
                pltpu.make_async_remote_copy(
                    src_ref=block,
                    dst_ref=target.at[my_slot],
                    send_sem=send_sem,
                    recv_sem=recv_sem,
                    device_id=(plane * inner + 2 * pair + s, my_bit),
                    device_id_type=MESH,
                ).start()

            if first and t == 0:
                pl.when(jnp.logical_not(to_self))(remote)

                @pl.when(to_self)
                def _():
                    pltpu.make_async_copy(block, target.at[my_slot], recv_sem).start()
            else:
                remote()

    def send_all(source, target, send_sem, recv_sem):
        send_chunk(0, source, target, send_sem, recv_sem, False)

        def more(chunk, c):
            send_chunk(chunk, source, target, send_sem, recv_sem, False)
            return c

        lax.fori_loop(1, pairs, more, 0)

    loads = [
        pltpu.make_async_copy(src, dst, sem_in.at[i])
        for i, (src, dst) in enumerate(
            [
                (offset_h, offset),
                (ids_h, ids),
                (fluid_h, fluid),
                (sphere_h, sphere),
                (tl_h, tl_s),
                (tl_h, tl_v),
                (cstate_h, cstate),
                (cinv_h, cinv),
            ]
        )
    ]
    for copy in loads:
        copy.start()

    bar = pltpu.get_barrier_semaphore()

    def greet(plane, pair):
        mate = plane * inner + 2 * pair + s
        pl.semaphore_signal(bar, inc=1, device_id=(mate, my_bit), device_id_type=MESH)

    def greet_chunk(chunk, c):
        pair = lax.rem(my_pair + chunk, pairs)
        for t in range(planes):
            greet(turns[t], pair)
        return c

    for t in range(1, planes):
        greet(turns[t], my_pair)
    lax.fori_loop(1, pairs, greet_chunk, 0)

    @pl.when(jnp.logical_not(to_self))
    def _():
        greet(my_plane, my_pair)

    pl.semaphore_signal(bar, inc=1, device_id=(d, other), device_id_type=MESH)

    loads[0].wait()
    loads[1].wait()

    def stage_o(i, c):
        for half in range(2):
            tile = 4 * i + 2 * s + half
            send_o[i, half, 0:3, :] = offset[:, pl.ds(pl.multiple_of(tile * TILE, TILE), TILE)]
            send_o[i, half, 3:4, :] = ids[pl.ds(tile, 1), :].astype(f32)
        return c

    lax.fori_loop(0, half_n, stage_o, 0, unroll=min(half_n, 4))

    loads[2].wait()

    def prep(b, c):
        tile = fluid[:, pl.ds(pl.multiple_of(b * TILE, TILE), TILE)]
        turned = jnp.transpose(tile * 2.0)
        for axis in range(3):
            fb[b, axis] = jnp.broadcast_to(turned[:, axis : axis + 1], (TILE, TILE))
        mass = tile[7:8]
        pm = tile[6:7] * mass
        centred = tile[0:3] - 0.5
        mx = mass * centred
        mv = mass * tile[3:6] - press_coef * (pm * centred)
        zero = jnp.zeros((5, TILE), f32)
        rows = jnp.concatenate(
            [
                jnp.broadcast_to(mass, (3, TILE)), zero,
                jnp.broadcast_to(pm, (3, TILE)), zero,
                mx, zero,
                mv, zero,
            ],
            axis=0,
        )
        hi, lo = split2(rows)
        fcol[b] = jnp.concatenate([hi, lo], axis=0).astype(bf16)
        return c

    lax.fori_loop(0, fluid_tiles, prep, 0, unroll=PREP_UNROLL)

    loads[3].wait()

    def stage_s(a, c):
        by_tile[a] = sphere[:, pl.ds(pl.multiple_of(a * TILE, TILE), TILE)]
        return c

    lax.fori_loop(0, 2 * n, stage_s, 0, unroll=8)

    differ = my_bit + s - 2 * my_bit * s
    pl.semaphore_wait(bar, half_n + differ)

    send_all(send_o, recv_o, sem_so, sem_ro)

    for i in (4, 5, 6, 7):
        loads[i].wait()

    def slot(t, c):
        a = tl_s[0, t]
        b = tl_s[1, t]
        spheres = by_tile[a]
        twice = spheres[0:3] * 2.0
        sep = twice[0:1] - fb[b, 0]
        d2 = sep * sep
        sep = twice[1:2] - fb[b, 1]
        d2 = d2 + sep * sep
        sep = twice[2:3] - fb[b, 2]
        d2 = d2 + sep * sep
        d2 = jnp.maximum(d2, 1e-30)
        fall = jnp.maximum(1.0 - d2 * lax.rsqrt(d2), 0.0)
        cube = fall * fall * fall
        hi = cube.astype(bf16)
        lo = (cube - hi.astype(f32)).astype(bf16)
        col = fcol[b]
        sums = jnp.dot(
            jnp.concatenate([col, col], axis=1),
            jnp.concatenate([hi, lo], axis=0),
            preferred_element_type=f32,
        )
        sums = sums[0:32] + sums[32:64]
        x3 = spheres[0:3] - 0.5
        p4 = press_coef * spheres[6:7]
        force = (
            sums[0:3] * (p4 * x3 - spheres[3:6])
            + (press_coef * x3) * sums[8:11]
            - p4 * sums[16:19]
            + sums[24:27]
        )
        terms[pl.ds(pl.multiple_of(t * 8, 8), 3), :] = force
        return c

    lax.fori_loop(0, slots, slot, 0, unroll=min(slots, SLOT_UNROLL))

    lists = tl_v[0:1, :]
    live = lax.broadcasted_iota(jnp.int32, (n, slots), 1) < cnt_s[0]
    row = lax.broadcasted_iota(jnp.int32, (n, slots), 0)
    tile_row = jnp.where(row < half_n, 4 * row, 4 * (row - half_n) + 1)

    def place(parity, out):
        match = jnp.where(
            live & (jnp.broadcast_to(lists, (n, slots)) == tile_row + 2 * parity), 1.0, 0.0
        ).astype(bf16)
        for axis in range(3):
            rows = terms[pl.ds(axis, slots, stride=8), :]
            hi, lo = split2(rows)
            out[axis] = jnp.dot(match, hi.astype(bf16), preferred_element_type=f32) + jnp.dot(
                match, lo.astype(bf16), preferred_element_type=f32
            )

    place(other, f_oth)
    swap_f = pltpu.make_async_remote_copy(
        src_ref=f_oth, dst_ref=f_in, send_sem=sem_ps.at[0], recv_sem=sem_pr.at[0],
        device_id=(d, other), device_id_type=MESH,
    )
    swap_f.start()
    place(s, f_own)
    swap_f.wait()

    def stage_f(i, c):
        for half in range(2):
            at = pl.ds(half * half_n + i, 1)
            for axis in range(3):
                send_f[i, half, axis : axis + 1, :] = f_own[axis, at, :] + f_in[axis, at, :]
        return c

    lax.fori_loop(0, half_n, stage_f, 0, unroll=min(half_n, 8))

    send_all(send_f, recv_f, sem_sf, sem_rf.at[my_pair])

    for r in range(6):
        for h in range(HI):
            cs8[r, h : h + 1, :] = cstate[r : r + 1, h * TILE : (h + 1) * TILE]
    for r in range(4):
        for h in range(HI):
            cs8[6 + r, h : h + 1, :] = cinv[r : r + 1, h * TILE : (h + 1) * TILE]

    pltpu.make_async_copy(recv_o, recv_o, sem_ro).wait()
    low_rows = lax.broadcasted_iota(jnp.int32, (TILE, TILE), 0).astype(f32)
    high_rows = lax.broadcasted_iota(jnp.int32, (HI, TILE), 0).astype(f32)

    def high_low(e, half):
        label = recv_o[e, half, 3:4, :]
        high = jnp.floor(label * (1.0 / TILE))
        return high, label - high * TILE

    def build(e, c):
        pieces = []
        for half in range(2):
            _, low = high_low(e, half)
            pieces.append(
                jnp.where(jnp.broadcast_to(low, (TILE, TILE)) == low_rows, 1.0, 0.0).astype(bf16)
            )
        hot[e] = jnp.concatenate(pieces, axis=1)
        return c

    lax.fori_loop(0, half_n, build, 0, unroll=2)

    def spread(e, half):
        high, _ = high_low(e, half)
        mask = row8(high) == high_rows
        force = [row8(recv_f[e, half, r : r + 1, :]) for r in range(3)]
        off = [row8(recv_o[e, half, r : r + 1, :]) for r in range(3)]
        load = force + [
            off[1] * force[2] - off[2] * force[1],
            off[2] * force[0] - off[0] * force[2],
            off[0] * force[1] - off[1] * force[0],
        ]
        load = [jnp.where(mask, x, 0.0) for x in load]
        parts = [split2(x) for x in load]
        return jnp.concatenate([p[0] for p in parts] + [p[1] for p in parts], axis=0).astype(bf16)

    def arrival(k):
        return lax.rem(my_pair - k + pairs, pairs)

    def group_in(k, acc):
        g = arrival(k)
        block = recv_f.at[pl.ds(g * planes, planes)]
        pltpu.make_async_copy(block, block, sem_rf.at[g]).wait()
        for i in range(planes):
            e = g * planes + i
            left = jnp.concatenate([spread(e, 0), spread(e, 1)], axis=1)
            acc = acc + lax.dot_general(
                left, hot[e], (((1,), (1,)), ((), ())), preferred_element_type=f32
            )
        return acc

    acc = lax.fori_loop(0, pairs, group_in, jnp.zeros((12 * HI, TILE), f32))

    tot_send[...] = acc[0 : 6 * HI, :] + acc[6 * HI : 12 * HI, :]
    swap_t = pltpu.make_async_remote_copy(
        src_ref=tot_send, dst_ref=tot_in, send_sem=sem_ps.at[1], recv_sem=sem_pr.at[1],
        device_id=(d, other), device_id_type=MESH,
    )
    swap_t.start()
    swap_t.wait()

    velocity = []
    for r in range(6):
        total = tot_send[r * HI : (r + 1) * HI, :] + tot_in[r * HI : (r + 1) * HI, :]
        value = cs8[r] + cs8[6 if r < 3 else 4 + r] * total
        if r == 2:
            value = value - gravity_step
        velocity.append(value)
        for h in range(HI):
            vel_out[r : r + 1, h * TILE : (h + 1) * TILE] = value[h : h + 1, :]
    parts = [split2(x) for x in velocity]
    vel8[...] = jnp.concatenate([p[0] for p in parts] + [p[1] for p in parts], axis=0).astype(bf16)

    def stage_v(e):
        got = jnp.dot(vel8[...], hot[e], preferred_element_type=f32)
        got = got[0 : 6 * HI] + got[6 * HI : 12 * HI]
        for half in range(2):
            cols = slice(half * TILE, (half + 1) * TILE)
            high, _ = high_low(e, half)
            mask = row8(high) == high_rows
            mine = [got[r * HI : (r + 1) * HI, cols] for r in range(6)]
            off = [row8(recv_o[e, half, r : r + 1, :]) for r in range(3)]
            for r in range(3):
                r1, r2 = (r + 1) % 3, (r + 2) % 3
                value = mine[r] + mine[3 + r1] * off[r2] - mine[3 + r2] * off[r1]
                send_v[e, half, r : r + 1, :] = jnp.sum(
                    jnp.where(mask, value, 0.0), axis=0, keepdims=True
                )

    def push_v(chunk, c):
        g = lax.rem(my_pair + chunk, pairs)
        for i in range(planes):
            stage_v(g * planes + i)
        send_chunk(chunk, send_v, recv_v, sem_sv, sem_rv.at[my_pair], True)
        return c

    push_v(0, 0)
    lax.fori_loop(1, pairs, push_v, 0)

    def swap_v(g):
        block = pl.ds(g * planes, planes)
        return pltpu.make_async_remote_copy(
            src_ref=recv_v.at[block], dst_ref=part_v.at[block],
            send_sem=sem_vs, recv_sem=sem_vr.at[g],
            device_id=(d, other), device_id_type=MESH,
        )

    def write(parity, ref, g):
        for plane in range(planes):
            owner = plane * inner + 2 * g + parity
            for half in range(2):
                first = pl.multiple_of((2 * owner + half) * TILE, TILE)
                sv_out[:, pl.ds(first, TILE)] = ref[g * planes + plane, half]

    def group_v(k, c):
        g = arrival(k)
        block = recv_v.at[pl.ds(g * planes, planes)]
        pltpu.make_async_copy(block, block, sem_rv.at[g]).wait()
        swap_v(g).start()
        write(s, recv_v, g)
        return c

    lax.fori_loop(0, pairs, group_v, 0)

    def group_p(k, c):
        g = arrival(k)
        block = part_v.at[pl.ds(g * planes, planes)]
        pltpu.make_async_copy(block, block, sem_vr.at[g]).wait()
        write(other, part_v, g)
        return c

    lax.fori_loop(0, pairs, group_p, 0)

    for ref, sem in ((send_o, sem_so), (send_f, sem_sf), (send_v, sem_sv)):
        block = ref.at[pl.ds(0, half_n - 1)]
        pltpu.make_async_copy(block, block, sem).wait()

    @pl.when(jnp.logical_not(to_self))
    def _():
        for ref, sem in ((send_o, sem_so), (send_f, sem_sf), (send_v, sem_sv)):
            pltpu.make_async_copy(ref.at[0], ref.at[0], sem).wait()

    pltpu.make_async_copy(recv_v, recv_v, sem_vs).wait()


def stay(x):
    return pltpu.with_memory_space_constraint(x, pltpu.HBM)


def per_device(
    fluid_state,
    sphere_state,
    sphere_offset,
    tile_list,
    tile_count,
    clump_ids,
    clump_state,
    clump_inverse,
):
    n = lax.axis_size("space")
    slots = tile_list.shape[0]
    fluid_tiles = fluid_state.shape[1] // TILE
    spheres = sphere_state.shape[1]
    clumps = clump_state.shape[1]
    inner = 16 if n >= 32 else 4 if n >= 8 else 2
    pairs = inner // 2
    lists = tile_list.T
    vmem = pl.BlockSpec(memory_space=pltpu.VMEM)
    hbm = pl.BlockSpec(memory_space=pltpu.HBM)
    dma = pltpu.SemaphoreType.DMA
    block3 = pltpu.VMEM((n // 2, 2, 3, TILE), f32)
    block4 = pltpu.VMEM((n // 2, 2, 4, TILE), f32)
    planes = pltpu.VMEM((3, n, TILE), f32)
    return pl.pallas_call(
        functools.partial(kernel, n, slots, fluid_tiles, inner),
        out_shape=(
            jax.ShapeDtypeStruct((6, clumps), f32),
            jax.ShapeDtypeStruct((3, spheres), f32),
        ),
        in_specs=[hbm, pl.BlockSpec(memory_space=pltpu.SMEM)] + [hbm] * 6,
        out_specs=(vmem, vmem),
        scratch_shapes=[
            pltpu.SMEM((2, slots), jnp.int32),
            pltpu.VMEM((2, slots), jnp.int32),
            pltpu.VMEM(fluid_state.shape, f32),
            pltpu.VMEM(sphere_state.shape, f32),
            pltpu.VMEM(sphere_offset.shape, f32),
            pltpu.VMEM((spheres // TILE, TILE), jnp.int32),
            pltpu.VMEM(clump_state.shape, f32),
            pltpu.VMEM(clump_inverse.shape, f32),
            pltpu.VMEM((fluid_tiles, 3, TILE, TILE), f32),
            pltpu.VMEM((fluid_tiles, 64, TILE), bf16),
            pltpu.VMEM((2 * n, 7, TILE), f32),
            pltpu.VMEM((slots * 8, TILE), f32),
            planes,
            planes,
            planes,
            block4,
            block4,
            block3,
            block3,
            block3,
            block3,
            block3,
            pltpu.VMEM((n // 2, TILE, 2 * TILE), bf16),
            pltpu.VMEM((6 * HI, TILE), f32),
            pltpu.VMEM((6 * HI, TILE), f32),
            pltpu.VMEM((10, HI, TILE), f32),
            pltpu.VMEM((12 * HI, TILE), bf16),
            dma((8,)),
            dma(()),
            dma(()),
            dma(()),
            dma((pairs,)),
            dma(()),
            dma((pairs,)),
            dma((2,)),
            dma((2,)),
            dma(()),
            dma((pairs,)),
        ],
        compiler_params=pltpu.CompilerParams(
            collective_id=0, has_side_effects=True, vmem_limit_bytes=40 << 20
        ),
        name="step",
    )(
        stay(lists),
        tile_count,
        stay(fluid_state),
        stay(sphere_state),
        stay(sphere_offset),
        stay(clump_ids.reshape(spheres // TILE, TILE)),
        stay(clump_state),
        stay(clump_inverse),
    )


def solution(mesh):
    in_specs = (
        P(None, "space"),
        P(None, "space"),
        P(None, "space"),
        P(("space", "sub"), None),
        P(("space", "sub")),
        P("space"),
        P(None, "space"),
        P(None, "space"),
    )
    out_specs = (P(None, "space"), P(None, "space"))
    return jax.shard_map(
        per_device, mesh=mesh, in_specs=in_specs, out_specs=out_specs, check_vma=False
    )
```

```python
import functools

import jax
import jax.numpy as jnp
from jax import lax
from jax.experimental import pallas as pl
from jax.experimental.pallas import tpu as pltpu
from jax.sharding import PartitionSpec as P

TILE = 128
SLOT_UNROLL = 32
PREP_UNROLL = 4
HI = 8

MESH = pl.DeviceIdType.MESH
f32 = jnp.float32
bf16 = jnp.bfloat16

press_coef = 4.0
gravity_step = 0.1


def split2(x):
    hi = x.astype(bf16).astype(f32)
    return hi, x - hi


def row8(row):
    return jnp.broadcast_to(row, (8, TILE))


def kernel(
    n,
    slots,
    fluid_tiles,
    inner,
    tl_h,
    cnt_s,
    fluid_h,
    sphere_h,
    offset_h,
    ids_h,
    cstate_h,
    cinv_h,
    vel_out,
    sv_out,
    tl_s,
    tl_v,
    fluid,
    sphere,
    offset,
    ids,
    cstate,
    cinv,
    fb,
    fcol,
    by_tile,
    terms,
    f_own,
    f_oth,
    f_in,
    send_o,
    recv_o,
    send_f,
    recv_f,
    send_v,
    recv_v,
    part_v,
    hot,
    tot_send,
    tot_in,
    cs8,
    vel8,
    sem_in,
    sem_so,
    sem_ro,
    sem_sf,
    sem_rf,
    sem_sv,
    sem_rv,
    sem_ps,
    sem_pr,
    sem_vs,
    sem_vr,
):
    d = lax.axis_index("space")
    s = lax.axis_index("sub")
    other = 1 - s
    planes = n // inner
    pairs = inner // 2
    half_n = n // 2
    my_plane = d // inner
    my_pair = lax.rem(d, inner) // 2
    my_bit = lax.rem(d, 2)
    my_slot = my_pair * planes + my_plane
    to_self = my_bit == s
    turns = [
        lax.rem(my_plane + ((t + 1) // 2) * (1 - 2 * ((t + 1) % 2)) + planes, planes)
        for t in range(planes)
    ]

    def send_chunk(chunk, source, target, send_sem, recv_sem, by_slot):
        pair = lax.rem(my_pair + chunk, pairs)
        first = isinstance(chunk, int) and chunk == 0
        for t in reversed(range(planes)):
            plane = turns[t]
            block = source.at[pair * planes + plane if by_slot else plane * pairs + pair]

            def remote():
                pltpu.make_async_remote_copy(
                    src_ref=block,
                    dst_ref=target.at[my_slot],
                    send_sem=send_sem,
                    recv_sem=recv_sem,
                    device_id=(plane * inner + 2 * pair + s, my_bit),
                    device_id_type=MESH,
                ).start()

            if first and t == 0:
                pl.when(jnp.logical_not(to_self))(remote)

                @pl.when(to_self)
                def _():
                    pltpu.make_async_copy(block, target.at[my_slot], recv_sem).start()
            else:
                remote()

    def send_all(source, target, send_sem, recv_sem):
        send_chunk(0, source, target, send_sem, recv_sem, False)

        def more(chunk, c):
            send_chunk(chunk, source, target, send_sem, recv_sem, False)
            return c

        lax.fori_loop(1, pairs, more, 0)

    loads = [
        pltpu.make_async_copy(src, dst, sem_in.at[i])
        for i, (src, dst) in enumerate(
            [
                (offset_h, offset),
                (ids_h, ids),
                (fluid_h, fluid),
                (sphere_h, sphere),
                (tl_h, tl_s),
                (tl_h, tl_v),
                (cstate_h, cstate),
                (cinv_h, cinv),
            ]
        )
    ]
    for copy in loads:
        copy.start()

    bar = pltpu.get_barrier_semaphore()

    def greet(plane, pair):
        mate = plane * inner + 2 * pair + s
        pl.semaphore_signal(bar, inc=1, device_id=(mate, my_bit), device_id_type=MESH)

    def greet_chunk(chunk, c):
        pair = lax.rem(my_pair + chunk, pairs)
        for t in range(planes):
            greet(turns[t], pair)
        return c

    for t in range(1, planes):
        greet(turns[t], my_pair)
    lax.fori_loop(1, pairs, greet_chunk, 0)

    @pl.when(jnp.logical_not(to_self))
    def _():
        greet(my_plane, my_pair)

    pl.semaphore_signal(bar, inc=1, device_id=(d, other), device_id_type=MESH)

    loads[0].wait()
    loads[1].wait()

    def stage_o(i, c):
        for half in range(2):
            tile = 4 * i + 2 * s + half
            send_o[i, half, 0:3, :] = offset[:, pl.ds(pl.multiple_of(tile * TILE, TILE), TILE)]
            send_o[i, half, 3:4, :] = ids[pl.ds(tile, 1), :].astype(f32)
        return c

    lax.fori_loop(0, half_n, stage_o, 0, unroll=min(half_n, 4))

    loads[2].wait()

    def prep(b, c):
        tile = fluid[:, pl.ds(pl.multiple_of(b * TILE, TILE), TILE)]
        turned = jnp.transpose(tile * 2.0)
        for axis in range(3):
            fb[b, axis] = jnp.broadcast_to(turned[:, axis : axis + 1], (TILE, TILE))
        mass = tile[7:8]
        pm = tile[6:7] * mass
        centred = tile[0:3] - 0.5
        mx = mass * centred
        mv = mass * tile[3:6] - press_coef * (pm * centred)
        zero = jnp.zeros((5, TILE), f32)
        rows = jnp.concatenate(
            [
                jnp.broadcast_to(mass, (3, TILE)), zero,
                jnp.broadcast_to(pm, (3, TILE)), zero,
                mx, zero,
                mv, zero,
            ],
            axis=0,
        )
        hi, lo = split2(rows)
        fcol[b] = jnp.concatenate([hi, lo], axis=0).astype(bf16)
        return c

    lax.fori_loop(0, fluid_tiles, prep, 0, unroll=PREP_UNROLL)

    loads[3].wait()

    def stage_s(a, c):
        by_tile[a] = sphere[:, pl.ds(pl.multiple_of(a * TILE, TILE), TILE)]
        return c

    lax.fori_loop(0, 2 * n, stage_s, 0, unroll=8)

    for i in (4, 5, 6, 7):
        loads[i].wait()

    def slot(t, c):
        a = tl_s[0, t]
        b = tl_s[1, t]
        spheres = by_tile[a]
        twice = spheres[0:3] * 2.0
        sep = twice[0:1] - fb[b, 0]
        d2 = sep * sep
        sep = twice[1:2] - fb[b, 1]
        d2 = d2 + sep * sep
        sep = twice[2:3] - fb[b, 2]
        d2 = d2 + sep * sep
        d2 = jnp.maximum(d2, 1e-30)
        fall = jnp.maximum(1.0 - d2 * lax.rsqrt(d2), 0.0)
        cube = fall * fall * fall
        hi = cube.astype(bf16)
        lo = (cube - hi.astype(f32)).astype(bf16)
        col = fcol[b]
        sums = jnp.dot(
            jnp.concatenate([col, col], axis=1),
            jnp.concatenate([hi, lo], axis=0),
            preferred_element_type=f32,
        )
        sums = sums[0:32] + sums[32:64]
        x3 = spheres[0:3] - 0.5
        p4 = press_coef * spheres[6:7]
        force = (
            sums[0:3] * (p4 * x3 - spheres[3:6])
            + (press_coef * x3) * sums[8:11]
            - p4 * sums[16:19]
            + sums[24:27]
        )
        terms[pl.ds(pl.multiple_of(t * 8, 8), 3), :] = force
        return c

    early = min(slots, 32)
    lax.fori_loop(0, early, slot, 0, unroll=min(early, SLOT_UNROLL))

    differ = my_bit + s - 2 * my_bit * s
    pl.semaphore_wait(bar, half_n + differ)

    send_all(send_o, recv_o, sem_so, sem_ro)

    lax.fori_loop(early, slots, slot, 0, unroll=min(max(slots - early, 1), SLOT_UNROLL))

    lists = tl_v[0:1, :]
    live = lax.broadcasted_iota(jnp.int32, (n, slots), 1) < cnt_s[0]
    row = lax.broadcasted_iota(jnp.int32, (n, slots), 0)
    tile_row = jnp.where(row < half_n, 4 * row, 4 * (row - half_n) + 1)

    def place(parity, out):
        match = jnp.where(
            live & (jnp.broadcast_to(lists, (n, slots)) == tile_row + 2 * parity), 1.0, 0.0
        ).astype(bf16)
        for axis in range(3):
            rows = terms[pl.ds(axis, slots, stride=8), :]
            hi, lo = split2(rows)
            out[axis] = jnp.dot(match, hi.astype(bf16), preferred_element_type=f32) + jnp.dot(
                match, lo.astype(bf16), preferred_element_type=f32
            )

    place(other, f_oth)
    swap_f = pltpu.make_async_remote_copy(
        src_ref=f_oth, dst_ref=f_in, send_sem=sem_ps.at[0], recv_sem=sem_pr.at[0],
        device_id=(d, other), device_id_type=MESH,
    )
    swap_f.start()
    place(s, f_own)
    swap_f.wait()

    def stage_f(i, c):
        for half in range(2):
            at = pl.ds(half * half_n + i, 1)
            for axis in range(3):
                send_f[i, half, axis : axis + 1, :] = f_own[axis, at, :] + f_in[axis, at, :]
        return c

    lax.fori_loop(0, half_n, stage_f, 0, unroll=min(half_n, 8))

    send_all(send_f, recv_f, sem_sf, sem_rf.at[my_pair])

    for r in range(6):
        for h in range(HI):
            cs8[r, h : h + 1, :] = cstate[r : r + 1, h * TILE : (h + 1) * TILE]
    for r in range(4):
        for h in range(HI):
            cs8[6 + r, h : h + 1, :] = cinv[r : r + 1, h * TILE : (h + 1) * TILE]

    pltpu.make_async_copy(recv_o, recv_o, sem_ro).wait()
    low_rows = lax.broadcasted_iota(jnp.int32, (TILE, TILE), 0).astype(f32)
    high_rows = lax.broadcasted_iota(jnp.int32, (HI, TILE), 0).astype(f32)

    def high_low(e, half):
        label = recv_o[e, half, 3:4, :]
        high = jnp.floor(label * (1.0 / TILE))
        return high, label - high * TILE

    def build(e, c):
        pieces = []
        for half in range(2):
            _, low = high_low(e, half)
            pieces.append(
                jnp.where(jnp.broadcast_to(low, (TILE, TILE)) == low_rows, 1.0, 0.0).astype(bf16)
            )
        hot[e] = jnp.concatenate(pieces, axis=1)
        return c

    lax.fori_loop(0, half_n, build, 0, unroll=2)

    def spread(e, half):
        high, _ = high_low(e, half)
        mask = row8(high) == high_rows
        force = [row8(recv_f[e, half, r : r + 1, :]) for r in range(3)]
        off = [row8(recv_o[e, half, r : r + 1, :]) for r in range(3)]
        load = force + [
            off[1] * force[2] - off[2] * force[1],
            off[2] * force[0] - off[0] * force[2],
            off[0] * force[1] - off[1] * force[0],
        ]
        load = [jnp.where(mask, x, 0.0) for x in load]
        parts = [split2(x) for x in load]
        return jnp.concatenate([p[0] for p in parts] + [p[1] for p in parts], axis=0).astype(bf16)

    def arrival(k):
        return lax.rem(my_pair - k + pairs, pairs)

    def group_in(k, acc):
        g = arrival(k)
        block = recv_f.at[pl.ds(g * planes, planes)]
        pltpu.make_async_copy(block, block, sem_rf.at[g]).wait()
        for i in range(planes):
            e = g * planes + i
            left = jnp.concatenate([spread(e, 0), spread(e, 1)], axis=1)
            acc = acc + lax.dot_general(
                left, hot[e], (((1,), (1,)), ((), ())), preferred_element_type=f32
            )
        return acc

    acc = lax.fori_loop(0, pairs, group_in, jnp.zeros((12 * HI, TILE), f32))

    tot_send[...] = acc[0 : 6 * HI, :] + acc[6 * HI : 12 * HI, :]
    swap_t = pltpu.make_async_remote_copy(
        src_ref=tot_send, dst_ref=tot_in, send_sem=sem_ps.at[1], recv_sem=sem_pr.at[1],
        device_id=(d, other), device_id_type=MESH,
    )
    swap_t.start()
    swap_t.wait()

    velocity = []
    for r in range(6):
        total = tot_send[r * HI : (r + 1) * HI, :] + tot_in[r * HI : (r + 1) * HI, :]
        value = cs8[r] + cs8[6 if r < 3 else 4 + r] * total
        if r == 2:
            value = value - gravity_step
        velocity.append(value)
        for h in range(HI):
            vel_out[r : r + 1, h * TILE : (h + 1) * TILE] = value[h : h + 1, :]
    parts = [split2(x) for x in velocity]
    vel8[...] = jnp.concatenate([p[0] for p in parts] + [p[1] for p in parts], axis=0).astype(bf16)

    def stage_v(e):
        got = jnp.dot(vel8[...], hot[e], preferred_element_type=f32)
        got = got[0 : 6 * HI] + got[6 * HI : 12 * HI]
        for half in range(2):
            cols = slice(half * TILE, (half + 1) * TILE)
            high, _ = high_low(e, half)
            mask = row8(high) == high_rows
            mine = [got[r * HI : (r + 1) * HI, cols] for r in range(6)]
            off = [row8(recv_o[e, half, r : r + 1, :]) for r in range(3)]
            for r in range(3):
                r1, r2 = (r + 1) % 3, (r + 2) % 3
                value = mine[r] + mine[3 + r1] * off[r2] - mine[3 + r2] * off[r1]
                send_v[e, half, r : r + 1, :] = jnp.sum(
                    jnp.where(mask, value, 0.0), axis=0, keepdims=True
                )

    def push_v(chunk, c):
        g = lax.rem(my_pair + chunk, pairs)
        for i in range(planes):
            stage_v(g * planes + i)
        send_chunk(chunk, send_v, recv_v, sem_sv, sem_rv.at[my_pair], True)
        return c

    push_v(0, 0)
    lax.fori_loop(1, pairs, push_v, 0)

    def swap_v(g):
        block = pl.ds(g * planes, planes)
        return pltpu.make_async_remote_copy(
            src_ref=recv_v.at[block], dst_ref=part_v.at[block],
            send_sem=sem_vs, recv_sem=sem_vr.at[g],
            device_id=(d, other), device_id_type=MESH,
        )

    def write(parity, ref, g):
        for plane in range(planes):
            owner = plane * inner + 2 * g + parity
            for half in range(2):
                first = pl.multiple_of((2 * owner + half) * TILE, TILE)
                sv_out[:, pl.ds(first, TILE)] = ref[g * planes + plane, half]

    def group_v(k, c):
        g = arrival(k)
        block = recv_v.at[pl.ds(g * planes, planes)]
        pltpu.make_async_copy(block, block, sem_rv.at[g]).wait()
        swap_v(g).start()
        write(s, recv_v, g)
        return c

    lax.fori_loop(0, pairs, group_v, 0)

    def group_p(k, c):
        g = arrival(k)
        block = part_v.at[pl.ds(g * planes, planes)]
        pltpu.make_async_copy(block, block, sem_vr.at[g]).wait()
        write(other, part_v, g)
        return c

    lax.fori_loop(0, pairs, group_p, 0)

    for ref, sem in ((send_o, sem_so), (send_f, sem_sf), (send_v, sem_sv)):
        block = ref.at[pl.ds(0, half_n - 1)]
        pltpu.make_async_copy(block, block, sem).wait()

    @pl.when(jnp.logical_not(to_self))
    def _():
        for ref, sem in ((send_o, sem_so), (send_f, sem_sf), (send_v, sem_sv)):
            pltpu.make_async_copy(ref.at[0], ref.at[0], sem).wait()

    pltpu.make_async_copy(recv_v, recv_v, sem_vs).wait()


def stay(x):
    return pltpu.with_memory_space_constraint(x, pltpu.HBM)


def per_device(
    fluid_state,
    sphere_state,
    sphere_offset,
    tile_list,
    tile_count,
    clump_ids,
    clump_state,
    clump_inverse,
):
    n = lax.axis_size("space")
    slots = tile_list.shape[0]
    fluid_tiles = fluid_state.shape[1] // TILE
    spheres = sphere_state.shape[1]
    clumps = clump_state.shape[1]
    inner = 16 if n >= 32 else 4 if n >= 8 else 2
    pairs = inner // 2
    lists = tile_list.T
    vmem = pl.BlockSpec(memory_space=pltpu.VMEM)
    hbm = pl.BlockSpec(memory_space=pltpu.HBM)
    dma = pltpu.SemaphoreType.DMA
    block3 = pltpu.VMEM((n // 2, 2, 3, TILE), f32)
    block4 = pltpu.VMEM((n // 2, 2, 4, TILE), f32)
    planes = pltpu.VMEM((3, n, TILE), f32)
    return pl.pallas_call(
        functools.partial(kernel, n, slots, fluid_tiles, inner),
        out_shape=(
            jax.ShapeDtypeStruct((6, clumps), f32),
            jax.ShapeDtypeStruct((3, spheres), f32),
        ),
        in_specs=[hbm, pl.BlockSpec(memory_space=pltpu.SMEM)] + [hbm] * 6,
        out_specs=(vmem, vmem),
        scratch_shapes=[
            pltpu.SMEM((2, slots), jnp.int32),
            pltpu.VMEM((2, slots), jnp.int32),
            pltpu.VMEM(fluid_state.shape, f32),
            pltpu.VMEM(sphere_state.shape, f32),
            pltpu.VMEM(sphere_offset.shape, f32),
            pltpu.VMEM((spheres // TILE, TILE), jnp.int32),
            pltpu.VMEM(clump_state.shape, f32),
            pltpu.VMEM(clump_inverse.shape, f32),
            pltpu.VMEM((fluid_tiles, 3, TILE, TILE), f32),
            pltpu.VMEM((fluid_tiles, 64, TILE), bf16),
            pltpu.VMEM((2 * n, 7, TILE), f32),
            pltpu.VMEM((slots * 8, TILE), f32),
            planes,
            planes,
            planes,
            block4,
            block4,
            block3,
            block3,
            block3,
            block3,
            block3,
            pltpu.VMEM((n // 2, TILE, 2 * TILE), bf16),
            pltpu.VMEM((6 * HI, TILE), f32),
            pltpu.VMEM((6 * HI, TILE), f32),
            pltpu.VMEM((10, HI, TILE), f32),
            pltpu.VMEM((12 * HI, TILE), bf16),
            dma((8,)),
            dma(()),
            dma(()),
            dma(()),
            dma((pairs,)),
            dma(()),
            dma((pairs,)),
            dma((2,)),
            dma((2,)),
            dma(()),
            dma((pairs,)),
        ],
        compiler_params=pltpu.CompilerParams(
            collective_id=0, has_side_effects=True, vmem_limit_bytes=40 << 20
        ),
        name="step",
    )(
        stay(lists),
        tile_count,
        stay(fluid_state),
        stay(sphere_state),
        stay(sphere_offset),
        stay(clump_ids.reshape(spheres // TILE, TILE)),
        stay(clump_state),
        stay(clump_inverse),
    )


def solution(mesh):
    in_specs = (
        P(None, "space"),
        P(None, "space"),
        P(None, "space"),
        P(("space", "sub"), None),
        P(("space", "sub")),
        P("space"),
        P(None, "space"),
        P(None, "space"),
    )
    out_specs = (P(None, "space"), P(None, "space"))
    return jax.shard_map(
        per_device, mesh=mesh, in_specs=in_specs, out_specs=out_specs, check_vma=False
    )
```

```python
import functools

import jax
import jax.numpy as jnp
from jax import lax
from jax.experimental import pallas as pl
from jax.experimental.pallas import tpu as pltpu
from jax.sharding import PartitionSpec as P

TILE = 128
SLOT_UNROLL = 32
PREP_UNROLL = 4
HI = 8

MESH = pl.DeviceIdType.MESH
f32 = jnp.float32
bf16 = jnp.bfloat16

press_coef = 4.0
gravity_step = 0.1


def split2(x):
    hi = x.astype(bf16).astype(f32)
    return hi, x - hi


def row8(row):
    return jnp.broadcast_to(row, (8, TILE))


def kernel(
    n,
    slots,
    fluid_tiles,
    inner,
    tl_h,
    cnt_s,
    fluid_h,
    sphere_h,
    offset_h,
    ids_h,
    cstate_h,
    cinv_h,
    vel_out,
    sv_out,
    tl_s,
    tl_v,
    fluid,
    sphere,
    offset,
    ids,
    cstate,
    cinv,
    fb,
    fcol,
    by_tile,
    terms,
    f_own,
    f_oth,
    f_in,
    send_o,
    recv_o,
    send_f,
    recv_f,
    send_v,
    recv_v,
    part_v,
    hot,
    tot_send,
    tot_in,
    cs8,
    vel8,
    sem_in,
    sem_so,
    sem_ro,
    sem_sf,
    sem_rf,
    sem_sv,
    sem_rv,
    sem_ps,
    sem_pr,
    sem_vs,
    sem_vr,
):
    d = lax.axis_index("space")
    s = lax.axis_index("sub")
    other = 1 - s
    planes = n // inner
    pairs = inner // 2
    half_n = n // 2
    my_plane = d // inner
    my_pair = lax.rem(d, inner) // 2
    my_bit = lax.rem(d, 2)
    my_slot = my_pair * planes + my_plane
    to_self = my_bit == s
    turns = [
        lax.rem(my_plane + ((t + 1) // 2) * (1 - 2 * ((t + 1) % 2)) + planes, planes)
        for t in range(planes)
    ]

    def send_chunk(chunk, source, target, send_sem, recv_sem, by_slot):
        pair = lax.rem(my_pair + chunk, pairs)
        first = isinstance(chunk, int) and chunk == 0
        for t in reversed(range(planes)):
            plane = turns[t]
            block = source.at[pair * planes + plane if by_slot else plane * pairs + pair]

            def remote():
                pltpu.make_async_remote_copy(
                    src_ref=block,
                    dst_ref=target.at[my_slot],
                    send_sem=send_sem,
                    recv_sem=recv_sem,
                    device_id=(plane * inner + 2 * pair + s, my_bit),
                    device_id_type=MESH,
                ).start()

            if first and t == 0:
                pl.when(jnp.logical_not(to_self))(remote)

                @pl.when(to_self)
                def _():
                    pltpu.make_async_copy(block, target.at[my_slot], recv_sem).start()
            else:
                remote()

    def send_all(source, target, send_sem, recv_sem):
        send_chunk(0, source, target, send_sem, recv_sem, False)

        def more(chunk, c):
            send_chunk(chunk, source, target, send_sem, recv_sem, False)
            return c

        lax.fori_loop(1, pairs, more, 0)

    loads = [
        pltpu.make_async_copy(src, dst, sem_in.at[i])
        for i, (src, dst) in enumerate(
            [
                (offset_h, offset),
                (ids_h, ids),
                (fluid_h, fluid),
                (sphere_h, sphere),
                (tl_h, tl_s),
                (tl_h, tl_v),
                (cstate_h, cstate),
                (cinv_h, cinv),
            ]
        )
    ]
    for copy in loads:
        copy.start()

    bar = pltpu.get_barrier_semaphore()

    def greet(plane, pair):
        mate = plane * inner + 2 * pair + s
        pl.semaphore_signal(bar, inc=1, device_id=(mate, my_bit), device_id_type=MESH)

    def greet_chunk(chunk, c):
        pair = lax.rem(my_pair + chunk, pairs)
        for t in range(planes):
            greet(turns[t], pair)
        return c

    for t in range(1, planes):
        greet(turns[t], my_pair)
    lax.fori_loop(1, pairs, greet_chunk, 0)

    @pl.when(jnp.logical_not(to_self))
    def _():
        greet(my_plane, my_pair)

    pl.semaphore_signal(bar, inc=1, device_id=(d, other), device_id_type=MESH)

    loads[0].wait()
    loads[1].wait()

    def stage_o(i, c):
        for half in range(2):
            tile = 4 * i + 2 * s + half
            send_o[i, half, 0:3, :] = offset[:, pl.ds(pl.multiple_of(tile * TILE, TILE), TILE)]
            send_o[i, half, 3:4, :] = ids[pl.ds(tile, 1), :].astype(f32)
        return c

    lax.fori_loop(0, half_n, stage_o, 0, unroll=min(half_n, 4))

    loads[2].wait()

    def prep(b, c):
        tile = fluid[:, pl.ds(pl.multiple_of(b * TILE, TILE), TILE)]
        turned = jnp.transpose(tile * 2.0)
        for axis in range(3):
            fb[b, axis] = jnp.broadcast_to(turned[:, axis : axis + 1], (TILE, TILE))
        mass = tile[7:8]
        pm = tile[6:7] * mass
        centred = tile[0:3] - 0.5
        mx = mass * centred
        mv = mass * tile[3:6] - press_coef * (pm * centred)
        zero = jnp.zeros((5, TILE), f32)
        rows = jnp.concatenate(
            [
                jnp.broadcast_to(mass, (3, TILE)), zero,
                jnp.broadcast_to(pm, (3, TILE)), zero,
                mx, zero,
                mv, zero,
            ],
            axis=0,
        )
        hi, lo = split2(rows)
        fcol[b] = jnp.concatenate([hi, lo], axis=0).astype(bf16)
        return c

    lax.fori_loop(0, fluid_tiles, prep, 0, unroll=PREP_UNROLL)

    loads[3].wait()

    def stage_s(a, c):
        by_tile[a] = sphere[:, pl.ds(pl.multiple_of(a * TILE, TILE), TILE)]
        return c

    lax.fori_loop(0, 2 * n, stage_s, 0, unroll=8)

    for i in (4, 5, 6, 7):
        loads[i].wait()

    def slot(t, c):
        a = tl_s[0, t]
        b = tl_s[1, t]
        spheres = by_tile[a]
        twice = spheres[0:3] * 2.0
        sep = twice[0:1] - fb[b, 0]
        d2 = sep * sep
        sep = twice[1:2] - fb[b, 1]
        d2 = d2 + sep * sep
        sep = twice[2:3] - fb[b, 2]
        d2 = d2 + sep * sep
        d2 = jnp.maximum(d2, 1e-30)
        fall = jnp.maximum(1.0 - d2 * lax.rsqrt(d2), 0.0)
        cube = fall * fall * fall
        hi = cube.astype(bf16)
        lo = (cube - hi.astype(f32)).astype(bf16)
        col = fcol[b]
        sums = jnp.dot(
            jnp.concatenate([col, col], axis=1),
            jnp.concatenate([hi, lo], axis=0),
            preferred_element_type=f32,
        )
        sums = sums[0:32] + sums[32:64]
        x3 = spheres[0:3] - 0.5
        p4 = press_coef * spheres[6:7]
        force = (
            sums[0:3] * (p4 * x3 - spheres[3:6])
            + (press_coef * x3) * sums[8:11]
            - p4 * sums[16:19]
            + sums[24:27]
        )
        terms[pl.ds(pl.multiple_of(t * 8, 8), 3), :] = force
        return c

    early = min(slots, 32)
    lax.fori_loop(0, early, slot, 0, unroll=min(early, SLOT_UNROLL))

    differ = my_bit + s - 2 * my_bit * s
    pl.semaphore_wait(bar, half_n + differ)

    send_all(send_o, recv_o, sem_so, sem_ro)

    lax.fori_loop(early, slots, slot, 0, unroll=min(max(slots - early, 1), SLOT_UNROLL))

    lists = tl_v[0:1, :]
    live = lax.broadcasted_iota(jnp.int32, (n, slots), 1) < cnt_s[0]
    row = lax.broadcasted_iota(jnp.int32, (n, slots), 0)
    tile_row = jnp.where(row < half_n, 4 * row, 4 * (row - half_n) + 1)

    def place(parity, out):
        match = jnp.where(
            live & (jnp.broadcast_to(lists, (n, slots)) == tile_row + 2 * parity), 1.0, 0.0
        ).astype(bf16)
        for axis in range(3):
            rows = terms[pl.ds(axis, slots, stride=8), :]
            hi, lo = split2(rows)
            out[axis] = jnp.dot(match, hi.astype(bf16), preferred_element_type=f32) + jnp.dot(
                match, lo.astype(bf16), preferred_element_type=f32
            )

    place(other, f_oth)
    swap_f = pltpu.make_async_remote_copy(
        src_ref=f_oth, dst_ref=f_in, send_sem=sem_ps.at[0], recv_sem=sem_pr.at[0],
        device_id=(d, other), device_id_type=MESH,
    )
    swap_f.start()
    place(s, f_own)
    swap_f.wait()

    def stage_f(i):
        for half in range(2):
            at = pl.ds(half * half_n + i, 1)
            for axis in range(3):
                send_f[i, half, axis : axis + 1, :] = f_own[axis, at, :] + f_in[axis, at, :]

    def push_f(chunk, c):
        pair = lax.rem(my_pair + chunk, pairs)
        for plane in range(planes):
            stage_f(plane * pairs + pair)
        send_chunk(chunk, send_f, recv_f, sem_sf, sem_rf.at[my_pair], False)
        return c

    push_f(0, 0)
    lax.fori_loop(1, pairs, push_f, 0)

    for r in range(6):
        for h in range(HI):
            cs8[r, h : h + 1, :] = cstate[r : r + 1, h * TILE : (h + 1) * TILE]
    for r in range(4):
        for h in range(HI):
            cs8[6 + r, h : h + 1, :] = cinv[r : r + 1, h * TILE : (h + 1) * TILE]

    pltpu.make_async_copy(recv_o, recv_o, sem_ro).wait()
    low_rows = lax.broadcasted_iota(jnp.int32, (TILE, TILE), 0).astype(f32)
    high_rows = lax.broadcasted_iota(jnp.int32, (HI, TILE), 0).astype(f32)

    def high_low(e, half):
        label = recv_o[e, half, 3:4, :]
        high = jnp.floor(label * (1.0 / TILE))
        return high, label - high * TILE

    def build(e, c):
        pieces = []
        for half in range(2):
            _, low = high_low(e, half)
            pieces.append(
                jnp.where(jnp.broadcast_to(low, (TILE, TILE)) == low_rows, 1.0, 0.0).astype(bf16)
            )
        hot[e] = jnp.concatenate(pieces, axis=1)
        return c

    lax.fori_loop(0, half_n, build, 0, unroll=2)

    def spread(e, half):
        high, _ = high_low(e, half)
        mask = row8(high) == high_rows
        force = [row8(recv_f[e, half, r : r + 1, :]) for r in range(3)]
        off = [row8(recv_o[e, half, r : r + 1, :]) for r in range(3)]
        load = force + [
            off[1] * force[2] - off[2] * force[1],
            off[2] * force[0] - off[0] * force[2],
            off[0] * force[1] - off[1] * force[0],
        ]
        load = [jnp.where(mask, x, 0.0) for x in load]
        parts = [split2(x) for x in load]
        return jnp.concatenate([p[0] for p in parts] + [p[1] for p in parts], axis=0).astype(bf16)

    def arrival(k):
        return lax.rem(my_pair - k + pairs, pairs)

    def group_in(k, acc):
        g = arrival(k)
        block = recv_f.at[pl.ds(g * planes, planes)]
        pltpu.make_async_copy(block, block, sem_rf.at[g]).wait()
        for i in range(planes):
            e = g * planes + i
            left = jnp.concatenate([spread(e, 0), spread(e, 1)], axis=1)
            acc = acc + lax.dot_general(
                left, hot[e], (((1,), (1,)), ((), ())), preferred_element_type=f32
            )
        return acc

    acc = lax.fori_loop(0, pairs, group_in, jnp.zeros((12 * HI, TILE), f32))

    tot_send[...] = acc[0 : 6 * HI, :] + acc[6 * HI : 12 * HI, :]
    swap_t = pltpu.make_async_remote_copy(
        src_ref=tot_send, dst_ref=tot_in, send_sem=sem_ps.at[1], recv_sem=sem_pr.at[1],
        device_id=(d, other), device_id_type=MESH,
    )
    swap_t.start()
    swap_t.wait()

    velocity = []
    for r in range(6):
        total = tot_send[r * HI : (r + 1) * HI, :] + tot_in[r * HI : (r + 1) * HI, :]
        value = cs8[r] + cs8[6 if r < 3 else 4 + r] * total
        if r == 2:
            value = value - gravity_step
        velocity.append(value)
        cs8[r] = value
    parts = [split2(x) for x in velocity]
    vel8[...] = jnp.concatenate([p[0] for p in parts] + [p[1] for p in parts], axis=0).astype(bf16)

    def stage_v(e):
        got = jnp.dot(vel8[...], hot[e], preferred_element_type=f32)
        got = got[0 : 6 * HI] + got[6 * HI : 12 * HI]
        for half in range(2):
            cols = slice(half * TILE, (half + 1) * TILE)
            high, _ = high_low(e, half)
            mask = row8(high) == high_rows
            mine = [got[r * HI : (r + 1) * HI, cols] for r in range(6)]
            off = [row8(recv_o[e, half, r : r + 1, :]) for r in range(3)]
            for r in range(3):
                r1, r2 = (r + 1) % 3, (r + 2) % 3
                value = mine[r] + mine[3 + r1] * off[r2] - mine[3 + r2] * off[r1]
                send_v[e, half, r : r + 1, :] = jnp.sum(
                    jnp.where(mask, value, 0.0), axis=0, keepdims=True
                )

    def push_v(chunk, c):
        g = lax.rem(my_pair + chunk, pairs)
        for i in range(planes):
            stage_v(g * planes + i)
        send_chunk(chunk, send_v, recv_v, sem_sv, sem_rv.at[my_pair], True)
        return c

    push_v(0, 0)
    lax.fori_loop(1, pairs, push_v, 0)

    for r in range(6):
        for h in range(HI):
            vel_out[r : r + 1, h * TILE : (h + 1) * TILE] = cs8[r, h : h + 1, :]

    def swap_v(g):
        block = pl.ds(g * planes, planes)
        return pltpu.make_async_remote_copy(
            src_ref=recv_v.at[block], dst_ref=part_v.at[block],
            send_sem=sem_vs, recv_sem=sem_vr.at[g],
            device_id=(d, other), device_id_type=MESH,
        )

    def write(parity, ref, g):
        for plane in range(planes):
            owner = plane * inner + 2 * g + parity
            for half in range(2):
                first = pl.multiple_of((2 * owner + half) * TILE, TILE)
                sv_out[:, pl.ds(first, TILE)] = ref[g * planes + plane, half]

    def group_v(k, c):
        g = arrival(k)
        block = recv_v.at[pl.ds(g * planes, planes)]
        pltpu.make_async_copy(block, block, sem_rv.at[g]).wait()
        swap_v(g).start()
        write(s, recv_v, g)
        return c

    lax.fori_loop(0, pairs, group_v, 0)

    def group_p(k, c):
        g = arrival(k)
        block = part_v.at[pl.ds(g * planes, planes)]
        pltpu.make_async_copy(block, block, sem_vr.at[g]).wait()
        write(other, part_v, g)
        return c

    lax.fori_loop(0, pairs, group_p, 0)

    for ref, sem in ((send_o, sem_so), (send_f, sem_sf), (send_v, sem_sv)):
        block = ref.at[pl.ds(0, half_n - 1)]
        pltpu.make_async_copy(block, block, sem).wait()

    @pl.when(jnp.logical_not(to_self))
    def _():
        for ref, sem in ((send_o, sem_so), (send_f, sem_sf), (send_v, sem_sv)):
            pltpu.make_async_copy(ref.at[0], ref.at[0], sem).wait()

    pltpu.make_async_copy(recv_v, recv_v, sem_vs).wait()


def stay(x):
    return pltpu.with_memory_space_constraint(x, pltpu.HBM)


def per_device(
    fluid_state,
    sphere_state,
    sphere_offset,
    tile_list,
    tile_count,
    clump_ids,
    clump_state,
    clump_inverse,
):
    n = lax.axis_size("space")
    slots = tile_list.shape[0]
    fluid_tiles = fluid_state.shape[1] // TILE
    spheres = sphere_state.shape[1]
    clumps = clump_state.shape[1]
    inner = 16 if n >= 32 else 4 if n >= 8 else 2
    pairs = inner // 2
    lists = tile_list.T
    vmem = pl.BlockSpec(memory_space=pltpu.VMEM)
    hbm = pl.BlockSpec(memory_space=pltpu.HBM)
    dma = pltpu.SemaphoreType.DMA
    block3 = pltpu.VMEM((n // 2, 2, 3, TILE), f32)
    block4 = pltpu.VMEM((n // 2, 2, 4, TILE), f32)
    planes = pltpu.VMEM((3, n, TILE), f32)
    return pl.pallas_call(
        functools.partial(kernel, n, slots, fluid_tiles, inner),
        out_shape=(
            jax.ShapeDtypeStruct((6, clumps), f32),
            jax.ShapeDtypeStruct((3, spheres), f32),
        ),
        in_specs=[hbm, pl.BlockSpec(memory_space=pltpu.SMEM)] + [hbm] * 6,
        out_specs=(vmem, vmem),
        scratch_shapes=[
            pltpu.SMEM((2, slots), jnp.int32),
            pltpu.VMEM((2, slots), jnp.int32),
            pltpu.VMEM(fluid_state.shape, f32),
            pltpu.VMEM(sphere_state.shape, f32),
            pltpu.VMEM(sphere_offset.shape, f32),
            pltpu.VMEM((spheres // TILE, TILE), jnp.int32),
            pltpu.VMEM(clump_state.shape, f32),
            pltpu.VMEM(clump_inverse.shape, f32),
            pltpu.VMEM((fluid_tiles, 3, TILE, TILE), f32),
            pltpu.VMEM((fluid_tiles, 64, TILE), bf16),
            pltpu.VMEM((2 * n, 7, TILE), f32),
            pltpu.VMEM((slots * 8, TILE), f32),
            planes,
            planes,
            planes,
            block4,
            block4,
            block3,
            block3,
            block3,
            block3,
            block3,
            pltpu.VMEM((n // 2, TILE, 2 * TILE), bf16),
            pltpu.VMEM((6 * HI, TILE), f32),
            pltpu.VMEM((6 * HI, TILE), f32),
            pltpu.VMEM((10, HI, TILE), f32),
            pltpu.VMEM((12 * HI, TILE), bf16),
            dma((8,)),
            dma(()),
            dma(()),
            dma(()),
            dma((pairs,)),
            dma(()),
            dma((pairs,)),
            dma((2,)),
            dma((2,)),
            dma(()),
            dma((pairs,)),
        ],
        compiler_params=pltpu.CompilerParams(
            collective_id=0, has_side_effects=True, vmem_limit_bytes=40 << 20
        ),
        name="step",
    )(
        stay(lists),
        tile_count,
        stay(fluid_state),
        stay(sphere_state),
        stay(sphere_offset),
        stay(clump_ids.reshape(spheres // TILE, TILE)),
        stay(clump_state),
        stay(clump_inverse),
    )


def solution(mesh):
    in_specs = (
        P(None, "space"),
        P(None, "space"),
        P(None, "space"),
        P(("space", "sub"), None),
        P(("space", "sub")),
        P("space"),
        P(None, "space"),
        P(None, "space"),
    )
    out_specs = (P(None, "space"), P(None, "space"))
    return jax.shard_map(
        per_device, mesh=mesh, in_specs=in_specs, out_specs=out_specs, check_vma=False
    )
```
